256 devices in a mesh: side: 2 (over core), grp: 32 (over z, y), tp: 4 (over x).
Axes of the slice: x: 4, y: 4, z: 8, core: 2. Of those that a mesh axis runs over, the one named last changes fastest.
Arguments:
- queries: bfloat16 [4096, 4096], P(('side', 'grp'), 'tp'), may hold values from -80 to 80
- new_key: bfloat16 [4096, 512], P(('side', 'grp'), 'tp'), may hold values from -4 to 4
- new_value: bfloat16 [4096, 512], P(('side', 'grp'), 'tp'), may hold values from -6 to 6
- key_cache: bfloat16 [4096, 128, 512], P(('side', 'grp'), None, 'tp'), may hold values from -5 to 5
- value_cache: bfloat16 [4096, 128, 512], P(('side', 'grp'), None, 'tp'), may hold values from -6 to 6
- cache_len: int32 [4096], P(('side', 'grp')), may hold values from 1 to 128, as said below
- residual: bfloat16 [4096, 4096], P(('side', 'grp'), 'tp'), may hold values from -30 to 30
- norm_gain: float32 [4096], replicated, may hold values from 0.5 to 1.5
- expert_ids: int32 [4096, 8], P(('side', 'grp')), may hold values from 0 to 127, all different within a row; in each aligned block of 64 rows (0 to 63, 64 to 127, ...) at most 8 rows name the same one
- gate_probs: float32 [4096, 8], P(('side', 'grp')), may hold values from 0.1 to 1
- w_gate: bfloat16 [128, 768, 4096], P(('side', 'grp'), 'tp'), may hold values from -0.09375 to 0.09375
- w_up: bfloat16 [128, 768, 4096], P(('side', 'grp'), 'tp'), may hold values from -0.09375 to 0.09375
- w_down: bfloat16 [128, 768, 4096], P(('side', 'grp'), 'tp'), may hold values from -0.21875 to 0.21875
Outputs:
- layer_out: bfloat16 [4096, 4096], P(('side', 'grp'), 'tp')
The draws below stay inside these ranges and needn't reach their ends.
Inputs may be any that keep to these rules, and one draw needn't show every extreme that they name: `cache_len`: some row's cache holds 128 tokens. `expert_ids`: A row names 8 different experts. Among the 64 rows of one device (aligned blocks of rows), no expert is named by more than 8 rows, and in some blocks one expert is named by exactly 8.
All inputs are finite; a program needn't handle non-finite values.
Results may differ from the reference program's by a relative error of at most 0.0085.
Values may be sent and summed in bfloat16 or wider, within the bound.
No kernel may reach another device: no remote copies, remote signals or barrier semaphores. Data moves between devices by JAX's collectives and lax.ppermute only.
A program may use at most 128 MiB of HBM per device.

```python
import math
import jax
import jax.numpy as jnp
import numpy as np
from jax import lax

D = 4096
HQ = 32
KVH = 4
HD = 128
F = 768
TOPK = 8
ROW_DEV = 64
CACHE = 128
ROWS = 4096
EXPERTS = 128
CAP = 8
N_TP = 4


def attention_inputs(key):
    base = jax.random.fold_in(key, 11)
    key_query, key_fresh, key_cached = jax.random.split(base, 3)
    fresh = jnp.clip(jax.random.normal(key_fresh, (ROWS, KVH, HD), jnp.float32), -4.0, 4.0)
    cached = jnp.clip(jax.random.normal(key_cached, (ROWS, CACHE, KVH, HD), jnp.float32), -5.0, 5.0)
    query_heads = jnp.clip(jax.random.normal(key_query, (ROWS, HQ, HD), jnp.float32), -6.0, 6.0)
    return (query_heads.reshape(ROWS, HQ * HD), fresh.reshape(ROWS, KVH * HD), cached.reshape(ROWS, CACHE, KVH * HD))


def draw_queries(key, part):
    return attention_inputs(key)[0].astype(jnp.bfloat16)


def draw_new_key(key, part):
    return attention_inputs(key)[1].astype(jnp.bfloat16)


def draw_key_cache(key, part):
    return attention_inputs(key)[2].astype(jnp.bfloat16)


def draw_cache_len(key, part):
    base = jax.random.fold_in(key, 23)
    key_ceiling, key_length, key_longest = jax.random.split(base, 3)
    blocks = ROWS // ROW_DEV
    ceiling = jax.random.randint(key_ceiling, (blocks, 1), CACHE // 8 + 1, CACHE + 1)
    lengths = jax.random.randint(key_length, (blocks, ROW_DEV), 1, ceiling + 1).reshape(ROWS)
    longest = jax.random.randint(key_longest, (), 0, ROWS)
    lengths = jnp.where(jnp.arange(ROWS) == longest, CACHE, lengths)
    return lengths.astype(jnp.int32)


def draw_residual(key, part):
    base = jax.random.fold_in(key, 31)
    key_base, key_row, key_col = jax.random.split(base, 3)
    row_scale = jnp.exp(jax.random.uniform(key_row, (ROWS, 1), jnp.float32, -2.3, 0.0))
    col_scale = jnp.exp(jax.random.uniform(key_col, (1, D), jnp.float32, -1.15, 1.15))
    drawn = jnp.clip(jax.random.normal(key_base, (ROWS, D), jnp.float32), -3.0, 3.0)
    values = drawn * row_scale * col_scale
    return jnp.clip(values, -30.0, 30.0).astype(jnp.bfloat16)


def steps_of(key, extent, pieces, low, high):
    def one(position, parts):
        heights = jax.random.uniform(jax.random.fold_in(jax.random.fold_in(key, 6), position), (parts,), jnp.float32, low / len(pieces), high / len(pieces))
        return jnp.repeat(jnp.exp(heights), extent[position] // parts).reshape((-1,) + (1,) * (len(extent) - position - 1))

    gain = one(*pieces[0])
    for cut in pieces[1:]:
        gain = gain * one(*cut)
    return gain


def shared_out(stream_key, own, number, rows, number_of, top, reach, skew):
    sequence = jax.random.permutation(stream_key, number_of)
    packed, common = shares(number_of, rows * top, reach, skew, True), shares(number_of, rows * top, reach, skew, False)
    places = jnp.arange(number_of)

    def named(tallies, turn):
        used = int((tallies > 0).sum())
        fixed = max(1, used // 4)
        passed = fixed + (places - fixed + turn * (used - fixed)) % max(1, number_of - fixed)
        return jnp.zeros((number_of,), jnp.int32).at[sequence[jnp.where(places < fixed, places, passed)]].set(jnp.asarray(tallies, jnp.int32))

    tallies = jnp.where(number % 4 == 0, named(packed, number // 4), named(common, number - number // 4 - 1))
    mixed = jax.random.permutation(jax.random.fold_in(own, 3), number_of)
    giver, taker = mixed[0:number_of // 2 * 2:2], mixed[1:number_of // 2 * 2:2]
    room = jnp.minimum(tallies[giver] - 1, reach - tallies[taker]) // 2
    room = jnp.where((giver == sequence[0]) | (taker == sequence[0]) | (tallies[taker] == 0), 0, jnp.maximum(room, 0))
    passed = jax.random.randint(jax.random.fold_in(own, 4), (number_of // 2,), 0, 1 << 20) % (room + 1)
    tallies = tallies.at[giver].add(-passed).at[taker].add(passed)
    items = jnp.searchsorted(jnp.cumsum(tallies), jnp.arange(rows * top), side="right").astype(jnp.int32)
    table = items.reshape(top, rows).T
    table = table[jax.random.permutation(jax.random.fold_in(own, 1), rows)]
    turn = jax.random.randint(jax.random.fold_in(own, 2), (rows, 1), 0, top)
    return jnp.take_along_axis(table, (jnp.arange(top)[None, :] + turn) % top, axis=1)


def shares(count, total, most, slope, full):
    weights = [(1 << 20) // math.isqrt(rank ** slope) + 1 for rank in range(1, count + 1)]
    largest = most if full else min(most, max(-(-total // count), total * weights[0] // sum(weights)))
    least = 1 if total - largest >= count - 1 else 0
    given, spare = [largest] + [least] * (count - 1), total - largest - least * (count - 1)
    while spare > 0:
        free = [i for i in range(1, count) if given[i] < largest] or [i for i in range(1, count) if given[i] < most]
        whole, left = sum([weights[i] for i in free]), spare
        for i in free:
            extra = min(most - given[i], max(1, left * weights[i] // whole), spare)
            given[i] = given[i] + extra
            spare = spare - extra
    return np.array(given)


def noise(own_key, dims, width, bound, cuts=(), kind=jnp.bfloat16):
    array = jax.random.normal(own_key, dims, jnp.float32) * width
    if len(cuts) > 0:
        array = steps_of(own_key, dims, cuts, -0.22, 0.18) * array
    return jnp.clip(array, min=-bound, max=bound).astype(kind)


def setup_inputs(seed: int = 0) -> dict:
    streams_of = jax.random.split(jax.random.key(seed), 14)
    queries = draw_queries(jax.random.fold_in(streams_of[13], 71), 0)
    new_key = draw_new_key(jax.random.fold_in(streams_of[13], 71), 0)
    new_value = noise(streams_of[2], (ROWS, KVH * HD), 1.0, 6.0, ((0, 64), (1, 4)))
    key_cache = draw_key_cache(jax.random.fold_in(streams_of[13], 71), 0)
    value_cache = noise(streams_of[4], (ROWS, CACHE, KVH * HD), 1.0, 6.0, ((0, 64), (2, 4)))
    cache_len = draw_cache_len(jax.random.fold_in(streams_of[13], 71), 0)
    residual = draw_residual(jax.random.fold_in(streams_of[13], 71), 0)
    norm_gain = jnp.clip(1.0 + 0.1 * jax.random.normal(streams_of[7], (D,), jnp.float32), 0.5, 1.5)
    expert_ids_keys = jax.random.split(jax.random.fold_in(streams_of[8], 1), ROWS // ROW_DEV)
    expert_ids_turns = jax.random.permutation(jax.random.fold_in(streams_of[8], 3), ROWS // ROW_DEV)
    expert_ids = jax.vmap(lambda own, number: shared_out(jax.random.fold_in(streams_of[8], 2), own, number, ROW_DEV, EXPERTS, TOPK, CAP, 2))(expert_ids_keys, expert_ids_turns).reshape((ROWS, TOPK))
    gate_probs = jnp.clip(jnp.exp(math.log(1.0) - 2.3025851 * jax.random.uniform(streams_of[9], (ROWS, TOPK), jnp.float32) ** steps_of(streams_of[9], (ROWS, TOPK), ((0, 64),), -0.2, 0.2)), 0.1, 1.0)
    w_gate = noise(streams_of[10], (EXPERTS, F, D), D ** -0.5, 0.09375, ((0, 64), (1, 4)))
    w_up = noise(streams_of[11], (EXPERTS, F, D), D ** -0.5, 0.09375, ((0, 64), (1, 4)))
    w_down = noise(streams_of[12], (EXPERTS, F, D), F ** -0.5, 0.21875, ((0, 64), (1, 4)))
    return dict(queries=queries, new_key=new_key, new_value=new_value, key_cache=key_cache, value_cache=value_cache, cache_len=cache_len, residual=residual, norm_gain=norm_gain, expert_ids=expert_ids, gate_probs=gate_probs, w_gate=w_gate, w_up=w_up, w_down=w_down)


epsilon = 1e-06

def reference(queries, new_key, new_value, key_cache, value_cache, cache_len, residual, norm_gain, expert_ids, gate_probs, w_gate, w_up, w_down):
    group_size = HQ // KVH
    blocks = ROWS // ROW_DEV
    query_heads = queries.astype(jnp.float32).reshape(ROWS, KVH, group_size, HD)
    cache_keys = key_cache.astype(jnp.float32).reshape(ROWS, CACHE, KVH, HD)
    cache_values = value_cache.astype(jnp.float32).reshape(ROWS, CACHE, KVH, HD)
    fresh_keys = new_key.astype(jnp.float32).reshape(ROWS, KVH, HD)
    fresh_values = new_value.astype(jnp.float32).reshape(ROWS, KVH, HD)
    score_scale = 1.0 / math.sqrt(HD)
    cache_scores = jnp.einsum('rkgd,rjkd->rkgj', query_heads, cache_keys) * score_scale
    live_mask = jnp.arange(CACHE).astype(jnp.int32)[None, :] < cache_len[:, None]
    cache_scores = jnp.where(live_mask[:, None, None, :], cache_scores, -jnp.inf)
    fresh_scores = jnp.einsum('rkgd,rkd->rkg', query_heads, fresh_keys) * score_scale
    top_score = jnp.maximum(lax.optimization_barrier(jnp.max(cache_scores, axis=-1)), fresh_scores)
    cache_exp = jnp.exp(cache_scores - top_score[..., None])
    fresh_exp = jnp.exp(fresh_scores - top_score)
    denominator = lax.optimization_barrier(jnp.sum(cache_exp, axis=-1)) + fresh_exp
    cache_weights = (cache_exp / denominator[..., None]).astype(jnp.bfloat16)
    fresh_weights = (fresh_exp / denominator).astype(jnp.bfloat16)
    attended = jnp.einsum('rkgj,rjkd->rkgd', cache_weights.astype(jnp.float32), cache_values)
    attended = attended + fresh_weights.astype(jnp.float32)[..., None] * fresh_values[:, :, None, :]
    attended = attended.reshape(ROWS, D)
    summed = residual.astype(jnp.float32) + attended
    mean_square = lax.optimization_barrier(jnp.mean(summed * summed, axis=-1, keepdims=True))
    normed = (summed * lax.rsqrt(mean_square + epsilon) * norm_gain).astype(jnp.bfloat16)
    mix = gate_probs / lax.optimization_barrier(jnp.sum(gate_probs, axis=-1, keepdims=True))
    expert_hits = lax.optimization_barrier(jnp.sum((expert_ids[:, :, None] == jnp.arange(EXPERTS).astype(jnp.int32)[None, None, :]).astype(jnp.int32), axis=1))
    per_block = expert_hits.reshape(blocks, ROW_DEV, EXPERTS)
    earlier = (jnp.cumsum(per_block, axis=1) - per_block).reshape(ROWS, EXPERTS).astype(jnp.int32)
    slot_rank = jnp.take_along_axis(earlier, expert_ids, axis=1).astype(jnp.int32)
    slot_index = (expert_ids * CAP + slot_rank).astype(jnp.int32)
    block_index = jnp.broadcast_to((jnp.arange(ROWS).astype(jnp.int32) // ROW_DEV)[:, None], (ROWS, TOPK)).astype(jnp.int32)
    buffer = jnp.zeros((EXPERTS * CAP, blocks, D), jnp.bfloat16)
    buffer = buffer.at[slot_index, block_index].set(jnp.broadcast_to(normed[:, None, :], (ROWS, TOPK, D)))
    buffer = buffer.reshape(EXPERTS, CAP * blocks, D)
    quarter = F // N_TP

    def run_expert(operands):
        slab, gate_rows, up_rows, down_rows = operands
        gate_proj = jnp.dot(slab, gate_rows.T, preferred_element_type=jnp.float32)
        up_proj = jnp.dot(slab, up_rows.T, preferred_element_type=jnp.float32)
        activation = (jax.nn.silu(gate_proj) * up_proj).astype(jnp.bfloat16)
        combined = jnp.zeros((slab.shape[0], D), jnp.float32)
        for block_number in range(N_TP):
            low = block_number * quarter
            partial_sum = jnp.dot(activation[:, low:low + quarter], down_rows[low:low + quarter], preferred_element_type=jnp.float32)
            combined = combined + lax.optimization_barrier(partial_sum.astype(jnp.bfloat16)).astype(jnp.float32)
        return combined.astype(jnp.bfloat16)
    expert_out = lax.map(run_expert, (buffer, w_gate, w_up, w_down))
    expert_flat = expert_out.reshape(EXPERTS * CAP, blocks, D)
    picked = expert_flat[slot_index, block_index]
    mixed = lax.optimization_barrier(jnp.sum(mix[:, :, None] * picked.astype(jnp.float32), axis=1))
    return (summed + mixed).astype(jnp.bfloat16)
```

```python
import functools
import math

import jax
import jax.numpy as jnp
from jax import lax
from jax.experimental import pallas as pl
from jax.experimental.pallas import tpu as pltpu
from jax.sharding import PartitionSpec as P

HD = 128
TOPK = 8
EXP_DEV = 2
N_TP = 4
SLOTS = 8

epsilon = 1e-06
F32 = jnp.float32
BF16 = jnp.bfloat16


def attention(queries, new_key, new_value, key_cache, value_cache, cache_len):
    row_count = queries.shape[0]
    head_count = queries.shape[1] // HD
    cache_span = key_cache.shape[1]
    query_heads = queries.reshape(row_count, head_count, HD)
    score_scale = 1.0 / math.sqrt(HD)
    cache_scores = (
        jnp.einsum("rgd,rjd->rgj", query_heads, key_cache, preferred_element_type=F32)
        * score_scale
    )
    live_mask = jnp.arange(cache_span)[None, :] < cache_len[:, None]
    cache_scores = jnp.where(live_mask[:, None, :], cache_scores, -jnp.inf)
    fresh_scores = (
        jnp.einsum("rgd,rd->rg", query_heads, new_key, preferred_element_type=F32) * score_scale
    )
    top_score = jnp.maximum(jnp.max(cache_scores, axis=-1), fresh_scores)
    cache_exp = jnp.exp(cache_scores - top_score[..., None])
    fresh_exp = jnp.exp(fresh_scores - top_score)
    denominator = jnp.sum(cache_exp, axis=-1) + fresh_exp
    cache_weights = (cache_exp / denominator[..., None]).astype(BF16)
    fresh_weights = (fresh_exp / denominator).astype(BF16)
    attended = jnp.einsum("rgj,rjd->rgd", cache_weights, value_cache, preferred_element_type=F32)
    attended = attended + fresh_weights.astype(F32)[..., None] * new_value.astype(F32)[:, None, :]
    return attended.reshape(row_count, head_count * HD)


def route_kernel(ids_ref, probs_ref, place0_ref, place1_ref, hi0_ref, hi1_ref, lo0_ref, lo1_ref):
    rows, experts = ids_ref.shape[0], EXP_DEV * place0_ref.shape[1] // SLOTS
    ids, probs = ids_ref[...], probs_ref[...]
    mix = probs / jnp.sum(probs, axis=1, keepdims=True)
    lane = lax.broadcasted_iota(jnp.int32, (rows, experts), 1)
    hits = jnp.zeros((rows, experts), F32)
    mixed = jnp.zeros((rows, experts), F32)
    for k in range(TOPK):
        same = ids[:, k : k + 1] == lane
        hits = hits + jnp.where(same, 1.0, 0.0)
        mixed = mixed + jnp.where(same, mix[:, k : k + 1], 0.0)
    before = lax.broadcasted_iota(jnp.int32, (rows, rows), 1) < lax.broadcasted_iota(
        jnp.int32, (rows, rows), 0
    )
    hits = hits.astype(BF16)
    earlier = jnp.dot(before.astype(F32).astype(BF16), hits, preferred_element_type=F32)
    earlier = earlier.astype(BF16)
    mix_hi = mixed.astype(BF16)
    mix_lo = (mixed - mix_hi.astype(F32)).astype(BF16)
    width = place0_ref.shape[1]
    slot = lax.broadcasted_iota(jnp.int32, (rows, width), 1) % SLOTS
    owner = lax.broadcasted_iota(jnp.int32, (experts, width), 1) // SLOTS
    expert = lax.broadcasted_iota(jnp.int32, (experts, width), 0)
    for j, (place_ref, hi_ref, lo_ref) in enumerate(
        ((place0_ref, hi0_ref, lo0_ref), (place1_ref, hi1_ref, lo1_ref))
    ):
        spread = jnp.where(expert == owner * EXP_DEV + j, 1.0, 0.0).astype(BF16)
        wide = functools.partial(jnp.dot, preferred_element_type=F32)
        chosen = (wide(hits, spread) > 0.5) & (
            wide(earlier, spread).astype(jnp.int32) == slot
        )
        place_ref[...] = jnp.where(chosen, 1.0, 0.0).astype(BF16)
        hi_ref[...] = jnp.where(chosen, wide(mix_hi, spread), 0.0).astype(BF16)
        lo_ref[...] = jnp.where(chosen, wide(mix_lo, spread), 0.0).astype(BF16)


def route(expert_ids, gate_probs, devices):
    rows = expert_ids.shape[0]
    shape = jax.ShapeDtypeStruct((rows, devices * SLOTS), BF16)
    return pl.pallas_call(
        route_kernel, out_shape=(shape,) * 6, name="route"
    )(expert_ids, gate_probs)


def split_kernel(me_ref, w_ref, *out_refs):
    part = out_refs[0].shape[2]
    for turn, out_ref in enumerate(out_refs):
        start = pl.multiple_of(lax.rem(me_ref[0] + turn, N_TP) * part, part)
        out_ref[...] = w_ref[:, :, pl.ds(start, part)]


def split_columns(me, w):
    count, hidden, width = w.shape
    part = width // N_TP
    return pl.pallas_call(
        split_kernel,
        grid_spec=pltpu.PrefetchScalarGridSpec(
            num_scalar_prefetch=1,
            grid=(count,),
            in_specs=[pl.BlockSpec((1, hidden, width), lambda e, m: (e, 0, 0))],
            out_specs=[pl.BlockSpec((1, hidden, part), lambda e, m: (e, 0, 0))] * N_TP,
        ),
        out_shape=[jax.ShapeDtypeStruct((count, hidden, part), w.dtype)] * N_TP,
        name="split_columns",
        cost_estimate=pl.CostEstimate(flops=0, bytes_accessed=4 * w.size, transcendentals=0),
    )(me, w)


RIGHT = [(i, (i + 1) % N_TP) for i in range(N_TP)]
LEFT = [(i, (i - 1) % N_TP) for i in range(N_TP)]
ACROSS = [(i, (i + 2) % N_TP) for i in range(N_TP)]


def exchange(blocks):
    own, for_right, for_across, for_left = blocks
    from_left = lax.ppermute(for_right, "tp", RIGHT)
    from_right = lax.ppermute(for_left, "tp", LEFT)
    return own, from_left, from_right, lax.ppermute(for_across, "tp", ACROSS)


def ring(x):
    half = x.shape[0] // 2
    from_left = lax.ppermute(x, "tp", RIGHT)
    from_right = lax.ppermute(x, "tp", LEFT)
    far_low = lax.ppermute(from_left[:half], "tp", RIGHT)
    far_high = lax.ppermute(from_right[half:], "tp", LEFT)
    return x, from_left, from_right, far_low, far_high


ORIGIN = (0, N_TP - 1, 1, 2)


def up_kernel(me_ref, own, left, right, low, high, gate_ref, up_ref, inv_ref, out_ref):
    part = own.shape[1]
    dims = (((1,), (1,)), ((), ()))

    def run(far):
        gate = up = squares = None
        for block, turn in zip((own, left, right, far), ORIGIN, strict=True):
            start = pl.multiple_of(lax.rem(me_ref[0] + turn, N_TP) * part, part)
            x = block[...]
            cols = pl.ds(start, part)
            g = lax.dot_general(x, gate_ref[0, :, cols], dims, preferred_element_type=F32)
            u = lax.dot_general(x, up_ref[0, :, cols], dims, preferred_element_type=F32)
            plain = x.astype(F32) * inv_ref[:, cols]
            s = jnp.sum(plain * plain, axis=1, keepdims=True)
            gate, up, squares = (g, u, s) if gate is None else (gate + g, up + u, squares + s)
        scale = lax.rsqrt(squares / (N_TP * part) + epsilon)
        gate, up = gate * scale, up * scale
        out_ref[...] = (gate / (1.0 + jnp.exp(-gate)) * up).astype(out_ref.dtype)

    @pl.when(pl.program_id(0) == 0)
    def _():
        run(low)

    @pl.when(pl.program_id(0) == 1)
    def _():
        run(high)


def up_project(me, blocks, w_gate, w_up, inv_gain, expert):
    rows, part = blocks[0].shape
    hidden, width = w_gate.shape[1:]
    half = rows // 2
    row = pl.BlockSpec((half, part), lambda i, m: (i, 0))
    far = pl.BlockSpec((half, part), lambda i, m: (0, 0))
    weight = pl.BlockSpec((1, hidden, width), lambda i, m: (expert, 0, 0))
    return pl.pallas_call(
        up_kernel,
        grid_spec=pltpu.PrefetchScalarGridSpec(
            num_scalar_prefetch=1,
            grid=(2,),
            in_specs=[row, row, row, far, far, weight, weight,
                      pl.BlockSpec((1, width), lambda i, m: (0, 0))],
            out_specs=pl.BlockSpec((half, hidden), lambda i, m: (i, 0)),
        ),
        out_shape=jax.ShapeDtypeStruct((rows, hidden), BF16),
        compiler_params=pltpu.CompilerParams(vmem_limit_bytes=40 << 20),
        cost_estimate=pl.CostEstimate(
            flops=4 * rows * width * hidden,
            bytes_accessed=2 * rows * width + 4 * hidden * width,
            transcendentals=rows * hidden,
        ),
        name="up_project",
    )(me, *blocks, w_gate, w_up, inv_gain)


def down_kernel(own, left, right, low, high, w0, w1, w2, w3, out_ref):
    def run(far):
        total = None
        for block, w_ref in zip((own, left, right, far), (w0, w1, w2, w3), strict=True):
            term = jnp.dot(block[...], w_ref[0], preferred_element_type=F32)
            total = term if total is None else total + term
        out_ref[...] = total.astype(out_ref.dtype)

    @pl.when(pl.program_id(0) == 0)
    def _():
        run(low)

    @pl.when(pl.program_id(0) == 1)
    def _():
        run(high)


def down_project(blocks, weights, expert):
    rows, hidden = blocks[0].shape
    part = weights[0].shape[2]
    half = rows // 2
    row = pl.BlockSpec((half, hidden), lambda i: (i, 0))
    far = pl.BlockSpec((half, hidden), lambda i: (0, 0))
    return pl.pallas_call(
        down_kernel,
        grid=(2,),
        in_specs=[row, row, row, far, far]
        + [pl.BlockSpec((1, hidden, part), lambda i: (expert, 0, 0))] * N_TP,
        out_specs=pl.BlockSpec((half, part), lambda i: (i, 0)),
        out_shape=jax.ShapeDtypeStruct((rows, part), BF16),
        compiler_params=pltpu.CompilerParams(vmem_limit_bytes=40 << 20),
        cost_estimate=pl.CostEstimate(
            flops=8 * rows * hidden * part,
            bytes_accessed=8 * rows * hidden + 8 * hidden * part + 2 * rows * part,
            transcendentals=0,
        ),
        name="down_project",
    )(*blocks, *weights)


def place_kernel(place_ref, rows_ref, *refs):
    out_ref = refs[-1]
    dims = (((0,), (0,)), ((), ()))
    out_ref[...] = lax.dot_general(
        place_ref[...], rows_ref[...], dims, preferred_element_type=F32
    ).astype(out_ref.dtype)


def place_rows(place, rows, *after):
    slots, part = place.shape[1], rows.shape[1]
    return pl.pallas_call(
        place_kernel,
        in_specs=[pl.BlockSpec(memory_space=pltpu.VMEM)] * 2
        + [pl.BlockSpec(memory_space=pl.ANY)] * len(after),
        out_shape=jax.ShapeDtypeStruct((slots, part), BF16),
        cost_estimate=pl.CostEstimate(
            flops=2 * place.size * part, bytes_accessed=4 * slots * part, transcendentals=0
        ),
        name="place_rows",
    )(place, rows, *after)


def combine_kernel(summed, hi0, lo0, hi1, lo1, back0, back1, out_ref):
    dot = functools.partial(jnp.dot, preferred_element_type=F32)
    total = summed[...]
    for hi, lo, back in ((hi0, lo0, back0), (hi1, lo1, back1)):
        values = back[...]
        total = total + (dot(hi[...], values) + dot(lo[...], values))
    out_ref[...] = total.astype(out_ref.dtype)


def combine(summed, hi0, lo0, hi1, lo1, back0, back1):
    rows, part = summed.shape
    steps = 4
    piece = part // steps
    slots = back0.shape[0]
    weight = pl.BlockSpec((rows, slots), lambda i: (0, 0))
    column = pl.BlockSpec((rows, piece), lambda i: (0, i))
    back = pl.BlockSpec((slots, piece), lambda i: (0, i))
    return pl.pallas_call(
        combine_kernel,
        grid=(steps,),
        in_specs=[column, weight, weight, weight, weight, back, back],
        out_specs=column,
        out_shape=jax.ShapeDtypeStruct((rows, part), BF16),
        name="combine",
    )(summed, hi0, lo0, hi1, lo1, back0, back1)


def body(
    queries, new_key, new_value, key_cache, value_cache, cache_len, residual,
    norm_gain, expert_ids, gate_probs, w_gate, w_up, w_down,
):
    rows, part = residual.shape
    group = ("side", "grp")
    devices = lax.axis_size("side") * lax.axis_size("grp")
    tp = lax.axis_index("tp")
    me = tp.astype(jnp.int32).reshape(1)
    place0, place1, hi0, hi1, lo0, lo1 = route(expert_ids, gate_probs, devices)
    attended = attention(queries, new_key, new_value, key_cache, value_cache, cache_len)
    summed = residual.astype(F32) + attended
    gain = lax.dynamic_slice(norm_gain, (tp * part,), (part,))
    scaled = (summed * gain[None, :]).astype(BF16)
    inv_gain = (1.0 / norm_gain).reshape(1, -1)
    swap = functools.partial(
        lax.all_to_all, axis_name=group, split_axis=0, concat_axis=0, tiled=True
    )
    moved = exchange(split_columns(me, w_down))
    backs = []
    arrived = [
        swap(place_rows(place0, scaled)), swap(place_rows(place1, scaled, *moved[1:]))
    ]
    for expert in range(EXP_DEV):
        activation = up_project(me, ring(arrived[expert]), w_gate, w_up, inv_gain, expert)
        produced = down_project(ring(activation), moved, expert)
        backs.append(swap(produced))
    return combine(summed, hi0, lo0, hi1, lo1, *backs)


def solution(mesh):
    in_specs = (
        P(("side", "grp"), "tp"),
        P(("side", "grp"), "tp"),
        P(("side", "grp"), "tp"),
        P(("side", "grp"), None, "tp"),
        P(("side", "grp"), None, "tp"),
        P(("side", "grp")),
        P(("side", "grp"), "tp"),
        P(),
        P(("side", "grp"), None),
        P(("side", "grp"), None),
        P(("side", "grp"), "tp", None),
        P(("side", "grp"), "tp", None),
        P(("side", "grp"), "tp", None),
    )
    out_specs = P(("side", "grp"), "tp")
    return jax.shard_map(body, mesh=mesh, in_specs=in_specs, out_specs=out_specs, check_vma=False)
```

```python
import functools
import math

import jax
import jax.numpy as jnp
from jax import lax
from jax.experimental import pallas as pl
from jax.experimental.pallas import tpu as pltpu
from jax.sharding import PartitionSpec as P

HD = 128
TOPK = 8
EXP_DEV = 2
N_TP = 4
SLOTS = 8

epsilon = 1e-06
FAR_WEIGHT = (1, 14)
F32 = jnp.float32
BF16 = jnp.bfloat16


RIGHT = [(i, (i + 1) % N_TP) for i in range(N_TP)]
LEFT = [(i, (i - 1) % N_TP) for i in range(N_TP)]
ACROSS = [(i, (i + 2) % N_TP) for i in range(N_TP)]
VMEM = pl.BlockSpec(memory_space=pltpu.VMEM)
ANY = pl.BlockSpec(memory_space=pl.ANY)
BIG = pltpu.CompilerParams(vmem_limit_bytes=20 << 20)
dot = functools.partial(jnp.dot, preferred_element_type=F32)


def route_kernel(ids_ref, probs_ref, *tables):
    slots, rows = tables[0].shape
    experts = EXP_DEV * slots // SLOTS
    ids, probs = ids_ref[...], probs_ref[...]
    mix = probs / jnp.sum(probs, axis=0, keepdims=True)
    line = lax.broadcasted_iota(jnp.int32, (experts, rows), 0)
    hits = jnp.zeros((experts, rows), F32)
    mixed = jnp.zeros((experts, rows), F32)
    for k in range(TOPK):
        same = ids[k : k + 1, :] == line
        hits = hits + jnp.where(same, 1.0, 0.0)
        mixed = mixed + jnp.where(same, mix[k : k + 1, :], 0.0)
    before = lax.broadcasted_iota(jnp.int32, (rows, rows), 0) < lax.broadcasted_iota(
        jnp.int32, (rows, rows), 1
    )
    hits = hits.astype(BF16)
    earlier = dot(hits, jnp.where(before, 1.0, 0.0).astype(BF16)).astype(BF16)
    mix_hi = mixed.astype(BF16)
    mix_lo = (mixed - mix_hi.astype(F32)).astype(BF16)
    slot = (lax.broadcasted_iota(jnp.int32, (slots, rows), 0) % SLOTS).astype(F32)
    owner = lax.broadcasted_iota(jnp.int32, (slots, experts), 0) // SLOTS
    expert = lax.broadcasted_iota(jnp.int32, (slots, experts), 1)

    def table(spread, tall):
        return (dot(spread, hits) > 0.5) & (dot(spread, earlier) == tall)

    for j in range(EXP_DEV):
        spread = jnp.where(expert == owner * EXP_DEV + j, 1.0, 0.0).astype(BF16)
        chosen = table(spread, slot)
        tables[j][...] = jnp.where(chosen, dot(spread, mix_hi), 0.0).astype(BF16)
        tables[2 + j][...] = jnp.where(chosen, dot(spread, mix_lo), 0.0).astype(BF16)
    for j in range(EXP_DEV):
        spread = jnp.where(expert == owner + j * (slots // SLOTS), 1.0, 0.0).astype(BF16)
        tables[4][pl.ds(j * slots, slots), :] = jnp.where(table(spread, slot), 1.0, 0.0).astype(BF16)


def route(ids, probs, devices):
    rows = ids.shape[1]
    table = jax.ShapeDtypeStruct((devices * SLOTS, rows), BF16)

    tall = jax.ShapeDtypeStruct((EXP_DEV * devices * SLOTS, rows), BF16)
    return pl.pallas_call(
        route_kernel,
        in_specs=[VMEM, VMEM],
        out_specs=[VMEM] * 5,
        out_shape=[table] * 4 + [tall],
        cost_estimate=pl.CostEstimate(
            flops=16 * devices * SLOTS * rows, bytes_accessed=0, transcendentals=0
        ),
        name="route",
    )(ids, probs)


def split_columns(me, w):
    count, hidden, width = w.shape
    part = width // N_TP
    block = pl.BlockSpec((1, hidden // 2, part), lambda h, m: (0, h, 0))
    shape = jax.ShapeDtypeStruct((1, hidden, part), w.dtype)

    def kernel(me_ref, w_ref, *out_refs):
        for e in range(count):
            for turn in range(1, N_TP):
                out_refs[e * (N_TP - 1) + turn - 1][0] = w_ref[e, :, columns(me_ref, turn, part)]

    return pl.pallas_call(
        kernel,
        grid_spec=pltpu.PrefetchScalarGridSpec(
            num_scalar_prefetch=1,
            grid=(2,),
            in_specs=[pl.BlockSpec((count, hidden // 2, width), lambda h, m: (0, h, 0))],
            out_specs=[block] * (count * (N_TP - 1)),
        ),
        out_shape=[shape] * (count * (N_TP - 1)),
        compiler_params=BIG,
        cost_estimate=pl.CostEstimate(flops=0, bytes_accessed=4 * w.size, transcendentals=0),
        name="split_columns",
    )(me, w)


def attention_kernel(
    lens_ref, q_ref, nk_ref, nv_ref, k_ref, v_ref, res_ref, gain_ref, summed_ref, scaled_ref
):
    rows, span, depth = k_ref.shape
    heads = q_ref.shape[1] // depth
    base = pl.program_id(0) * rows
    lines = rows * heads
    q = q_ref[...].astype(F32).reshape(rows, heads, depth)
    qb = q.astype(BF16)
    dims = (((1,), (1,)), ((), ()))
    scores = jnp.concatenate(
        [
            lax.dot_general(qb[r], k_ref[r], dims, preferred_element_type=F32)
            for r in range(rows)
        ],
        axis=0,
    )
    scale = 1.0 / math.sqrt(depth)
    line = lax.broadcasted_iota(jnp.int32, (lines, span), 0) // heads
    limit = jnp.zeros((lines, span), jnp.int32)
    for r in range(rows):
        limit = jnp.where(line == r, lens_ref[base + r], limit)
    live = lax.broadcasted_iota(jnp.int32, (lines, span), 1) < limit
    scores = jnp.where(live, scores * scale, -jnp.inf)
    fresh_key = jnp.broadcast_to(nk_ref[...].astype(F32)[:, None, :], (rows, heads, depth))
    fresh = jnp.sum(q * fresh_key, axis=2, keepdims=True).reshape(lines, 1) * scale
    top = jnp.maximum(jnp.max(scores, axis=1, keepdims=True), fresh)
    exps = jnp.exp(scores - top)
    fresh_exp = jnp.exp(fresh - top)
    total = jnp.sum(exps, axis=1, keepdims=True) + fresh_exp
    weights = (exps / total).astype(BF16)
    fresh_weight = (fresh_exp / total).astype(BF16).astype(F32)
    fresh_value = jnp.broadcast_to(nv_ref[...].astype(F32)[:, None, :], (rows, heads, depth))
    out = jnp.concatenate(
        [dot(weights[r * heads : (r + 1) * heads], v_ref[r]) for r in range(rows)], axis=0
    )
    out = out + fresh_weight * fresh_value.reshape(lines, depth)
    summed = res_ref[...].astype(F32) + out.reshape(rows, heads, depth).reshape(
        rows, heads * depth
    )
    summed_ref[...] = summed
    scaled_ref[...] = (summed * gain_ref[...]).astype(BF16)


def attention(lens, me, queries, new_key, new_value, keys, values, residual, gain):
    rows, part = queries.shape
    span, depth = keys.shape[1:]
    step = 16
    wide = pl.BlockSpec((step, part), lambda i, n, m: (i, 0))
    slim = pl.BlockSpec((step, depth), lambda i, n, m: (i, 0))
    cache = pl.BlockSpec((step, span, depth), lambda i, n, m: (i, 0, 0))

    def kernel(lens_ref, me_ref, *refs):
        attention_kernel(lens_ref, *refs)

    return pl.pallas_call(
        kernel,
        grid_spec=pltpu.PrefetchScalarGridSpec(
            num_scalar_prefetch=2,
            grid=(rows // step,),
            in_specs=[wide, slim, slim, cache, cache, wide,
                      pl.BlockSpec((1, part), lambda i, n, m: (0, m[0]))],
            out_specs=[wide, wide],
        ),
        out_shape=[
            jax.ShapeDtypeStruct((rows, part), F32), jax.ShapeDtypeStruct((rows, part), BF16)
        ],
        compiler_params=pltpu.CompilerParams(vmem_limit_bytes=58 << 20),
        cost_estimate=pl.CostEstimate(
            flops=4 * rows * part * span,
            bytes_accessed=4 * rows * span * depth,
            transcendentals=rows * part,
        ),
        name="attention",
    )(lens, me, queries, new_key, new_value, keys, values, residual, gain)


def place_kernel(table_ref, rows_ref, out_ref):
    out_ref[...] = dot(table_ref[...], rows_ref[...]).astype(BF16)


def place_rows(table, rows):
    slots, part = table.shape[0], rows.shape[1]
    return pl.pallas_call(
        place_kernel,
        grid=(2,),
        in_specs=[
            pl.BlockSpec((slots // 2, table.shape[1]), lambda i: (i, 0)),
            pl.BlockSpec(rows.shape, lambda i: (0, 0)),
        ],
        out_specs=pl.BlockSpec((slots // 2, part), lambda i: (i, 0)),
        out_shape=jax.ShapeDtypeStruct((slots, part), BF16),
        cost_estimate=pl.CostEstimate(
            flops=2 * table.size * part, bytes_accessed=4 * slots * part, transcendentals=0
        ),
        name="place_rows",
    )(table, rows)


def pick_kernel(all_ref, *refs):
    for i, out_ref in enumerate(refs[-2:]):
        count = all_ref.shape[0] // 2
        out_ref[...] = all_ref[pl.ds(i * count, count)].reshape(out_ref.shape)


def pick(everything, expert, *after):
    devices, _, slots, part = everything.shape
    half = devices * slots // 2
    return pl.pallas_call(
        pick_kernel,
        grid=(1,),
        in_specs=[pl.BlockSpec((devices, 1, slots, part), lambda i: (0, expert, 0, 0))]
        + [ANY] * len(after),
        out_specs=[pl.BlockSpec((half, part), lambda i: (0, 0))] * 2,
        out_shape=[jax.ShapeDtypeStruct((half, part), everything.dtype)] * 2,
        cost_estimate=pl.CostEstimate(
            flops=0, bytes_accessed=8 * half * part, transcendentals=0
        ),
        name="pick",
    )(everything, *after)


def in_hbm(*arrays):
    return [pltpu.with_memory_space_constraint(array, pltpu.HBM) for array in arrays]


def exchange(for_right, for_across, for_left):
    return (
        lax.ppermute(for_right, "tp", RIGHT),
        lax.ppermute(for_left, "tp", LEFT),
        lax.ppermute(for_across, "tp", ACROSS),
    )


def columns(me_ref, turn, part):
    return pl.ds(pl.multiple_of(lax.rem(me_ref[0] + turn, N_TP) * part, part), part)


def project(x, cols, gate_ref, up_ref, inv_ref):
    dims = (((1,), (1,)), ((), ()))
    plain = x.astype(F32) * inv_ref[:, cols]
    return (
        lax.dot_general(x, gate_ref[0, :, cols], dims, preferred_element_type=F32),
        lax.dot_general(x, up_ref[0, :, cols], dims, preferred_element_type=F32),
        jnp.sum(plain * plain, axis=1, keepdims=True),
    )


def near_kernel(
    me_ref, own0, own1, left0, left1, right0, right1, gate_ref, up_ref, inv_ref,
    gate_out, up_out, sq_out,
):
    half, part = own0.shape
    for i, blocks in enumerate(((own0, left0, right0), (own1, left1, right1))):
        rows = pl.ds(i * half, half)
        total = None
        for block, turn in zip(blocks, (0, N_TP - 1, 1), strict=True):
            term = project(block[...], columns(me_ref, turn, part), gate_ref, up_ref, inv_ref)
            total = term if total is None else tuple(
                a + b for a, b in zip(total, term, strict=True)
            )
        gate_out[rows, :], up_out[rows, :] = total[0], total[1]
        sq_out[rows, :] = jnp.broadcast_to(total[2], (half, sq_out.shape[1]))


def far_kernel(me_ref, low, high, gate_in, up_in, sq_in, gate_ref, up_ref, inv_ref, out_ref):
    half, part = low.shape
    hidden = gate_in.shape[1]
    tails = []
    for i, block in enumerate((low, high)):
        rows = slice(i * half, (i + 1) * half)
        cols = pl.ds(0, part)
        gate, up, squares = project(block[...], cols, gate_ref, up_ref, inv_ref)
        scale = lax.rsqrt((sq_in[rows, :1] + squares) / (N_TP * part) + epsilon)
        gate, up = (gate_in[rows] + gate) * scale, (up_in[rows] + up) * scale
        value = gate / (1.0 + jnp.exp(-gate)) * up
        out_ref[rows, :] = value[:, :128].astype(BF16)
        tails.append(value[:, 128:hidden])
    out_ref[2 * half :, :] = jnp.concatenate(tails, axis=1).astype(BF16)


def near_project(me, blocks, w_gate, w_up, inv_gain, expert):
    rows, part = 2 * blocks[0].shape[0], blocks[0].shape[1]
    hidden, width = w_gate.shape[1:]

    def whole(shape):
        return pl.BlockSpec(shape, lambda i, m: (0,) * len(shape))

    weight = pl.BlockSpec((1, hidden, width), lambda i, m: (expert, 0, 0))
    return pl.pallas_call(
        near_kernel,
        grid_spec=pltpu.PrefetchScalarGridSpec(
            num_scalar_prefetch=1,
            grid=(1,),
            in_specs=[whole(blocks[0].shape)] * 6 + [weight, weight, whole((1, width))],
            out_specs=[whole((rows, hidden)), whole((rows, hidden)), whole((rows, 128))],
        ),
        out_shape=[jax.ShapeDtypeStruct((rows, hidden), F32)] * 2
        + [jax.ShapeDtypeStruct((rows, 128), F32)],
        compiler_params=pltpu.CompilerParams(vmem_limit_bytes=32 << 20),
        cost_estimate=pl.CostEstimate(
            flops=3 * rows * width * hidden,
            bytes_accessed=2 * rows * width + 4 * hidden * width,
            transcendentals=0,
        ),
        name="near_project",
    )(me, *blocks, w_gate, w_up, inv_gain)


def far_project(me, low, high, near, w_gate, w_up, inv_gain, expert, weight_us):
    half, part = low.shape
    hidden, width = w_gate.shape[1:]
    rows = 2 * half

    def whole(shape):
        return pl.BlockSpec(shape, lambda i, m: (0,) * len(shape))

    def across(m):
        return lax.rem(m[0] + 2, N_TP)

    weight = pl.BlockSpec((1, hidden, part), lambda i, m: (expert, 0, across(m)))
    packed = (rows + rows * (hidden - 128) // 128, 128)

    return pl.pallas_call(
        far_kernel,
        grid_spec=pltpu.PrefetchScalarGridSpec(
            num_scalar_prefetch=1,
            grid=(1,),
            in_specs=[whole(low.shape), whole(high.shape)]
            + [whole(a.shape) for a in near]
            + [weight, weight, pl.BlockSpec((1, part), lambda i, m: (0, across(m)))],
            out_specs=whole(packed),
        ),
        out_shape=jax.ShapeDtypeStruct(packed, BF16),
        compiler_params=BIG,
        cost_estimate=pl.CostEstimate(
            flops=int(weight_us * 1e9), bytes_accessed=8 * rows * part, transcendentals=0
        ),
        name="far_project",
    )(me, low, high, *near, w_gate, w_up, inv_gain)


def down_kernel(me_ref, h0, h1, h2, h3, w0, w1, w2, w3, out_ref, *plain):
    rows, hidden = plain[0].shape

    @pl.when(pl.program_id(0) == 0)
    def _():
        for packed, full in zip((h0, h1, h2, h3), plain, strict=True):
            tails = packed[rows:, :]
            full[:, :128] = packed[:rows, :]
            full[: rows // 2, 128:] = tails[:, : hidden - 128]
            full[rows // 2 :, 128:] = tails[:, hidden - 128 :]

    total = None
    for full, w_ref in zip(plain, (w0, w1, w2, w3), strict=True):
        term = dot(full[...], w_ref[0])
        total = term if total is None else total + term
    out_ref[...] = total.astype(out_ref.dtype)


def down_project(me, packed, w_down, moved, rows, expert, *after):
    _, hidden, part = moved[0].shape
    whole = pl.BlockSpec(packed[0].shape, lambda i, m: (0, 0))
    steps = 2
    piece = part // steps
    own = pl.BlockSpec((1, hidden, piece), lambda i, m: (expert, 0, m[0] * steps + i))
    other = pl.BlockSpec((1, hidden, piece), lambda i, m: (0, 0, i))

    def kernel(*refs):
        head = 1 + 2 * N_TP
        down_kernel(*refs[:head], *refs[head + len(after) :])

    return pl.pallas_call(
        kernel,
        grid_spec=pltpu.PrefetchScalarGridSpec(
            num_scalar_prefetch=1,
            grid=(steps,),
            in_specs=[whole] * N_TP + [own] + [other] * (N_TP - 1) + [ANY] * len(after),
            out_specs=pl.BlockSpec((rows, piece), lambda i, m: (0, i)),
            scratch_shapes=[pltpu.VMEM((rows, hidden), BF16)] * N_TP,
        ),
        out_shape=pltpu.HBM((rows, part), BF16),
        compiler_params=BIG,
        cost_estimate=pl.CostEstimate(
            flops=8 * rows * hidden * part,
            bytes_accessed=8 * rows * hidden + 8 * hidden * part + 2 * rows * part,
            transcendentals=0,
        ),
        name="down_project",
    )(me, *packed, w_down, *moved, *after)


def mix_kernel(total_ref, hi_ref, lo_ref, back_ref, out_ref):
    back = back_ref[...]
    total = total_ref[...].astype(F32)
    for weight in (hi_ref, lo_ref):
        total = total + dot(weight[...], back)
    out_ref[...] = total.astype(out_ref.dtype)


def mix_in(total, hi, lo, back, dtype):
    rows, part = total.shape
    steps = 2
    column = pl.BlockSpec((rows, part // steps), lambda i: (0, i))
    weight = pl.BlockSpec(hi.shape, lambda i: (0, 0))
    return pl.pallas_call(
        mix_kernel,
        grid=(steps,),
        in_specs=[column, weight, weight,
                  pl.BlockSpec((back.shape[0], part // steps), lambda i: (0, i))],
        out_specs=column,
        out_shape=jax.ShapeDtypeStruct((rows, part), dtype),
        cost_estimate=pl.CostEstimate(
            flops=4 * hi.size * part, bytes_accessed=2 * back.size, transcendentals=0
        ),
        name="mix_in",
    )(total, hi, lo, back)


def body(
    queries, new_key, new_value, key_cache, value_cache, cache_len, residual,
    norm_gain, expert_ids, gate_probs, w_gate, w_up, w_down,
):
    rows, part = residual.shape
    group = ("side", "grp")
    devices = lax.axis_size("side") * lax.axis_size("grp")
    slots = devices * SLOTS
    me = lax.axis_index("tp").astype(jnp.int32).reshape(1)
    hi0, hi1, lo0, lo1, table = route(expert_ids.T, gate_probs.T, devices)
    blocks = split_columns(me, w_down)
    gain = norm_gain.reshape(1, -1)
    inv_gain = 1.0 / gain
    summed, scaled = attention(
        cache_len, me, queries, new_key, new_value, key_cache, value_cache, residual, gain
    )
    swap = functools.partial(
        lax.all_to_all, axis_name=group, split_axis=0, concat_axis=0, tiled=True
    )
    moved = [exchange(*blocks[: N_TP - 1]), exchange(*blocks[N_TP - 1 :])]
    moved[0] = in_hbm(*moved[0])
    w_gate, w_up = in_hbm(w_gate, w_up)
    arrived = swap(place_rows(table, scaled).reshape(devices, EXP_DEV, SLOTS, part))
    total = summed
    for expert, hi, lo in ((0, hi0, lo0), (1, hi1, lo1)):
        own = pick(arrived, expert, *moved[0], *moved[1])
        left = [lax.ppermute(half, "tp", RIGHT) for half in own]
        right = [lax.ppermute(half, "tp", LEFT) for half in own]
        low = lax.ppermute(left[0], "tp", RIGHT)
        high = lax.ppermute(right[1], "tp", LEFT)
        sums = near_project(me, (*own, *left, *right), w_gate, w_up, inv_gain, expert)
        packed = far_project(
            me, low, high, sums, w_gate, w_up, inv_gain, expert, FAR_WEIGHT[expert]
        )
        packed = packed, *exchange(packed, packed, packed)
        produced = down_project(me, packed, w_down, moved[expert], slots, expert)
        back = swap(produced.reshape(devices, SLOTS, part)).reshape(slots, part)
        total = mix_in(total, hi.T, lo.T, back, F32 if expert == 0 else BF16)
    return total


def solution(mesh):
    in_specs = (
        P(("side", "grp"), "tp"),
        P(("side", "grp"), "tp"),
        P(("side", "grp"), "tp"),
        P(("side", "grp"), None, "tp"),
        P(("side", "grp"), None, "tp"),
        P(("side", "grp")),
        P(("side", "grp"), "tp"),
        P(),
        P(("side", "grp"), None),
        P(("side", "grp"), None),
        P(("side", "grp"), "tp", None),
        P(("side", "grp"), "tp", None),
        P(("side", "grp"), "tp", None),
    )
    out_specs = P(("side", "grp"), "tp")
    return jax.shard_map(body, mesh=mesh, in_specs=in_specs, out_specs=out_specs, check_vma=False)
```

```python
import functools
import math

import jax
import jax.numpy as jnp
from jax import lax
from jax.experimental import pallas as pl
from jax.experimental.pallas import tpu as pltpu
from jax.sharding import PartitionSpec as P

HD = 128
TOPK = 8
EXP_DEV = 2
N_TP = 4
SLOTS = 8

epsilon = 1e-06
PICK_WEIGHT = (20, 0)
FAR_WEIGHT = (1, 14)
F32 = jnp.float32
BF16 = jnp.bfloat16


RIGHT = [(i, (i + 1) % N_TP) for i in range(N_TP)]
LEFT = [(i, (i - 1) % N_TP) for i in range(N_TP)]
ACROSS = [(i, (i + 2) % N_TP) for i in range(N_TP)]
VMEM = pl.BlockSpec(memory_space=pltpu.VMEM)
ANY = pl.BlockSpec(memory_space=pl.ANY)
BIG = pltpu.CompilerParams(vmem_limit_bytes=20 << 20)
dot = functools.partial(jnp.dot, preferred_element_type=F32)


def route_kernel(ids_ref, probs_ref, *tables):
    slots, rows = tables[0].shape
    experts = EXP_DEV * slots // SLOTS
    ids, probs = ids_ref[...], probs_ref[...]
    mix = probs / jnp.sum(probs, axis=0, keepdims=True)
    line = lax.broadcasted_iota(jnp.int32, (experts, rows), 0)
    hits = jnp.zeros((experts, rows), F32)
    mixed = jnp.zeros((experts, rows), F32)
    for k in range(TOPK):
        same = ids[k : k + 1, :] == line
        hits = hits + jnp.where(same, 1.0, 0.0)
        mixed = mixed + jnp.where(same, mix[k : k + 1, :], 0.0)
    before = lax.broadcasted_iota(jnp.int32, (rows, rows), 0) < lax.broadcasted_iota(
        jnp.int32, (rows, rows), 1
    )
    hits = hits.astype(BF16)
    earlier = dot(hits, jnp.where(before, 1.0, 0.0).astype(BF16)).astype(BF16)
    mix_hi = mixed.astype(BF16)
    mix_lo = (mixed - mix_hi.astype(F32)).astype(BF16)
    slot = (lax.broadcasted_iota(jnp.int32, (slots, rows), 0) % SLOTS).astype(F32)
    owner = lax.broadcasted_iota(jnp.int32, (slots, experts), 0) // SLOTS
    expert = lax.broadcasted_iota(jnp.int32, (slots, experts), 1)

    def table(spread, tall):
        return (dot(spread, hits) > 0.5) & (dot(spread, earlier) == tall)

    for j in range(EXP_DEV):
        spread = jnp.where(expert == owner * EXP_DEV + j, 1.0, 0.0).astype(BF16)
        chosen = table(spread, slot)
        tables[j][...] = jnp.where(chosen, dot(spread, mix_hi), 0.0).astype(BF16)
        tables[2 + j][...] = jnp.where(chosen, dot(spread, mix_lo), 0.0).astype(BF16)
        tables[4 + j][...] = jnp.where(chosen, 1.0, 0.0).astype(BF16)


def route(ids, probs, devices):
    rows = ids.shape[1]
    table = jax.ShapeDtypeStruct((devices * SLOTS, rows), BF16)

    return pl.pallas_call(
        route_kernel,
        in_specs=[VMEM, VMEM],
        out_specs=[VMEM] * 6,
        out_shape=[table] * 6,
        cost_estimate=pl.CostEstimate(
            flops=16 * devices * SLOTS * rows, bytes_accessed=0, transcendentals=0
        ),
        name="route",
    )(ids, probs)


def split_columns(me, w):
    count, hidden, width = w.shape
    part = width // N_TP
    block = pl.BlockSpec((1, hidden // 2, part), lambda h, m: (0, h, 0))
    shape = jax.ShapeDtypeStruct((1, hidden, part), w.dtype)

    def kernel(me_ref, w_ref, *out_refs):
        for e in range(count):
            for turn in range(1, N_TP):
                out_refs[e * (N_TP - 1) + turn - 1][0] = w_ref[e, :, columns(me_ref, turn, part)]

    return pl.pallas_call(
        kernel,
        grid_spec=pltpu.PrefetchScalarGridSpec(
            num_scalar_prefetch=1,
            grid=(2,),
            in_specs=[pl.BlockSpec((count, hidden // 2, width), lambda h, m: (0, h, 0))],
            out_specs=[block] * (count * (N_TP - 1)),
        ),
        out_shape=[shape] * (count * (N_TP - 1)),
        compiler_params=BIG,
        cost_estimate=pl.CostEstimate(flops=0, bytes_accessed=4 * w.size, transcendentals=0),
        name="split_columns",
    )(me, w)


def attention_kernel(
    lens_ref, q_ref, nk_ref, nv_ref, k_ref, v_ref, res_ref, gain_ref, summed_ref, scaled_ref
):
    rows, span, depth = k_ref.shape
    heads = q_ref.shape[1] // depth
    base = pl.program_id(0) * rows
    lines = rows * heads
    q = q_ref[...].astype(F32).reshape(rows, heads, depth)
    qb = q.astype(BF16)
    dims = (((1,), (1,)), ((), ()))
    scores = jnp.concatenate(
        [
            lax.dot_general(qb[r], k_ref[r], dims, preferred_element_type=F32)
            for r in range(rows)
        ],
        axis=0,
    )
    scale = 1.0 / math.sqrt(depth)
    line = lax.broadcasted_iota(jnp.int32, (lines, span), 0) // heads
    limit = jnp.zeros((lines, span), jnp.int32)
    for r in range(rows):
        limit = jnp.where(line == r, lens_ref[base + r], limit)
    live = lax.broadcasted_iota(jnp.int32, (lines, span), 1) < limit
    scores = jnp.where(live, scores * scale, -jnp.inf)
    fresh_key = jnp.broadcast_to(nk_ref[...].astype(F32)[:, None, :], (rows, heads, depth))
    fresh = jnp.sum(q * fresh_key, axis=2, keepdims=True).reshape(lines, 1) * scale
    top = jnp.maximum(jnp.max(scores, axis=1, keepdims=True), fresh)
    exps = jnp.exp(scores - top)
    fresh_exp = jnp.exp(fresh - top)
    total = jnp.sum(exps, axis=1, keepdims=True) + fresh_exp
    weights = (exps / total).astype(BF16)
    fresh_weight = (fresh_exp / total).astype(BF16).astype(F32)
    fresh_value = jnp.broadcast_to(nv_ref[...].astype(F32)[:, None, :], (rows, heads, depth))
    out = jnp.concatenate(
        [dot(weights[r * heads : (r + 1) * heads], v_ref[r]) for r in range(rows)], axis=0
    )
    out = out + fresh_weight * fresh_value.reshape(lines, depth)
    summed = res_ref[...].astype(F32) + out.reshape(rows, heads, depth).reshape(
        rows, heads * depth
    )
    summed_ref[...] = summed
    scaled_ref[...] = (summed * gain_ref[...]).astype(BF16)


def attention(lens, me, queries, new_key, new_value, keys, values, residual, gain):
    rows, part = queries.shape
    span, depth = keys.shape[1:]
    step = 32
    wide = pl.BlockSpec((step, part), lambda i, n, m: (i, 0))
    slim = pl.BlockSpec((step, depth), lambda i, n, m: (i, 0))
    cache = pl.BlockSpec((step, span, depth), lambda i, n, m: (i, 0, 0))

    def kernel(lens_ref, me_ref, *refs):
        attention_kernel(lens_ref, *refs)

    return pl.pallas_call(
        kernel,
        grid_spec=pltpu.PrefetchScalarGridSpec(
            num_scalar_prefetch=2,
            grid=(rows // step,),
            in_specs=[wide, slim, slim, cache, cache, wide,
                      pl.BlockSpec((1, part), lambda i, n, m: (0, m[0]))],
            out_specs=[wide, wide],
        ),
        out_shape=[
            jax.ShapeDtypeStruct((rows, part), F32), jax.ShapeDtypeStruct((rows, part), BF16)
        ],
        compiler_params=pltpu.CompilerParams(vmem_limit_bytes=58 << 20),
        cost_estimate=pl.CostEstimate(
            flops=4 * rows * part * span,
            bytes_accessed=4 * rows * span * depth,
            transcendentals=rows * part,
        ),
        name="attention",
    )(lens, me, queries, new_key, new_value, keys, values, residual, gain)


def place_kernel(table_ref, rows_ref, *refs):
    refs[-1][...] = dot(table_ref[...], rows_ref[...]).astype(BF16)


def place_rows(table, rows, *after):
    slots, part = table.shape[0], rows.shape[1]
    return pl.pallas_call(
        place_kernel,
        grid=(2,),
        in_specs=[
            pl.BlockSpec((slots // 2, table.shape[1]), lambda i: (i, 0)),
            pl.BlockSpec(rows.shape, lambda i: (0, 0)),
        ]
        + [ANY] * len(after),
        out_specs=pl.BlockSpec((slots // 2, part), lambda i: (i, 0)),
        out_shape=jax.ShapeDtypeStruct((slots, part), BF16),
        cost_estimate=pl.CostEstimate(
            flops=2 * table.size * part, bytes_accessed=4 * slots * part, transcendentals=0
        ),
        name="place_rows",
    )(table, rows, *after)


def pick_kernel(all_ref, *refs):
    for i, out_ref in enumerate(refs[-2:]):
        count = all_ref.shape[0] // 2
        out_ref[...] = all_ref[pl.ds(i * count, count)].reshape(out_ref.shape)


def pick(everything, expert, work, *after):
    devices, _, slots, part = everything.shape
    half = devices * slots // 2
    return pl.pallas_call(
        pick_kernel,
        grid=(1,),
        in_specs=[pl.BlockSpec((devices, 1, slots, part), lambda i: (0, expert, 0, 0))]
        + [ANY] * len(after),
        out_specs=[pl.BlockSpec((half, part), lambda i: (0, 0))] * 2,
        out_shape=[jax.ShapeDtypeStruct((half, part), everything.dtype)] * 2,
        compiler_params=BIG,
        cost_estimate=pl.CostEstimate(
            flops=int(work * 1e9), bytes_accessed=8 * half * part, transcendentals=0
        ),
        name="pick",
    )(everything, *after)


def in_hbm(*arrays):
    return [pltpu.with_memory_space_constraint(array, pltpu.HBM) for array in arrays]


def exchange(for_right, for_across, for_left):
    return (
        lax.ppermute(for_right, "tp", RIGHT),
        lax.ppermute(for_left, "tp", LEFT),
        lax.ppermute(for_across, "tp", ACROSS),
    )


def columns(me_ref, turn, part):
    return pl.ds(pl.multiple_of(lax.rem(me_ref[0] + turn, N_TP) * part, part), part)


def project(x, cols, gate_ref, up_ref, inv_ref):
    dims = (((1,), (1,)), ((), ()))
    plain = x.astype(F32) * inv_ref[:, cols]
    return (
        lax.dot_general(x, gate_ref[0, :, cols], dims, preferred_element_type=F32),
        lax.dot_general(x, up_ref[0, :, cols], dims, preferred_element_type=F32),
        jnp.sum(plain * plain, axis=1, keepdims=True),
    )


def near_kernel(
    me_ref, own0, own1, left0, left1, right0, right1, gate_ref, up_ref, inv_ref,
    gate_out, up_out, sq_out,
):
    half, part = own0.shape
    for i, blocks in enumerate(((own0, left0, right0), (own1, left1, right1))):
        rows = pl.ds(i * half, half)
        total = None
        for block, turn in zip(blocks, (0, N_TP - 1, 1), strict=True):
            term = project(block[...], columns(me_ref, turn, part), gate_ref, up_ref, inv_ref)
            total = term if total is None else tuple(
                a + b for a, b in zip(total, term, strict=True)
            )
        gate_out[rows, :], up_out[rows, :] = total[0], total[1]
        sq_out[rows, :] = jnp.broadcast_to(total[2], (half, sq_out.shape[1]))


def far_kernel(me_ref, low, high, gate_in, up_in, sq_in, gate_ref, up_ref, inv_ref, out_ref):
    half, part = low.shape
    hidden = gate_in.shape[1]
    tails = []
    for i, block in enumerate((low, high)):
        rows = slice(i * half, (i + 1) * half)
        cols = pl.ds(0, part)
        gate, up, squares = project(block[...], cols, gate_ref, up_ref, inv_ref)
        scale = lax.rsqrt((sq_in[rows, :1] + squares) / (N_TP * part) + epsilon)
        gate, up = (gate_in[rows] + gate) * scale, (up_in[rows] + up) * scale
        value = gate / (1.0 + jnp.exp(-gate)) * up
        out_ref[rows, :] = value[:, :128].astype(BF16)
        tails.append(value[:, 128:hidden])
    out_ref[2 * half :, :] = jnp.concatenate(tails, axis=1).astype(BF16)


def near_project(me, blocks, w_gate, w_up, inv_gain, expert):
    rows, part = 2 * blocks[0].shape[0], blocks[0].shape[1]
    hidden, width = w_gate.shape[1:]

    def whole(shape):
        return pl.BlockSpec(shape, lambda i, m: (0,) * len(shape))

    weight = pl.BlockSpec((1, hidden, width), lambda i, m: (expert, 0, 0))
    return pl.pallas_call(
        near_kernel,
        grid_spec=pltpu.PrefetchScalarGridSpec(
            num_scalar_prefetch=1,
            grid=(1,),
            in_specs=[whole(blocks[0].shape)] * 6 + [weight, weight, whole((1, width))],
            out_specs=[whole((rows, hidden)), whole((rows, hidden)), whole((rows, 128))],
        ),
        out_shape=[jax.ShapeDtypeStruct((rows, hidden), F32)] * 2
        + [jax.ShapeDtypeStruct((rows, 128), F32)],
        compiler_params=pltpu.CompilerParams(vmem_limit_bytes=32 << 20),
        cost_estimate=pl.CostEstimate(
            flops=3 * rows * width * hidden,
            bytes_accessed=2 * rows * width + 4 * hidden * width,
            transcendentals=0,
        ),
        name="near_project",
    )(me, *blocks, w_gate, w_up, inv_gain)


def far_project(me, low, high, near, w_gate, w_up, inv_gain, expert, weight_us):
    half, part = low.shape
    hidden, width = w_gate.shape[1:]
    rows = 2 * half

    def whole(shape):
        return pl.BlockSpec(shape, lambda i, m: (0,) * len(shape))

    def across(m):
        return lax.rem(m[0] + 2, N_TP)

    weight = pl.BlockSpec((1, hidden, part), lambda i, m: (expert, 0, across(m)))
    packed = (rows + rows * (hidden - 128) // 128, 128)

    return pl.pallas_call(
        far_kernel,
        grid_spec=pltpu.PrefetchScalarGridSpec(
            num_scalar_prefetch=1,
            grid=(1,),
            in_specs=[whole(low.shape), whole(high.shape)]
            + [whole(a.shape) for a in near]
            + [weight, weight, pl.BlockSpec((1, part), lambda i, m: (0, across(m)))],
            out_specs=whole(packed),
        ),
        out_shape=jax.ShapeDtypeStruct(packed, BF16),
        compiler_params=BIG,
        cost_estimate=pl.CostEstimate(
            flops=int(weight_us * 1e9), bytes_accessed=8 * rows * part, transcendentals=0
        ),
        name="far_project",
    )(me, low, high, *near, w_gate, w_up, inv_gain)


def down_kernel(me_ref, h0, h1, h2, h3, w0, w1, w2, w3, out_ref, *plain):
    rows, hidden = plain[0].shape

    @pl.when(pl.program_id(0) == 0)
    def _():
        for packed, full in zip((h0, h1, h2, h3), plain, strict=True):
            tails = packed[rows:, :]
            full[:, :128] = packed[:rows, :]
            full[: rows // 2, 128:] = tails[:, : hidden - 128]
            full[rows // 2 :, 128:] = tails[:, hidden - 128 :]

    total = None
    for full, w_ref in zip(plain, (w0, w1, w2, w3), strict=True):
        term = dot(full[...], w_ref[0])
        total = term if total is None else total + term
    out_ref[...] = total.astype(out_ref.dtype)


def down_project(me, packed, w_down, moved, rows, expert, *after):
    _, hidden, part = moved[0].shape
    whole = pl.BlockSpec(packed[0].shape, lambda i, m: (0, 0))
    steps = 2
    piece = part // steps
    own = pl.BlockSpec((1, hidden, piece), lambda i, m: (expert, 0, m[0] * steps + i))
    other = pl.BlockSpec((1, hidden, piece), lambda i, m: (0, 0, i))

    def kernel(*refs):
        head = 1 + 2 * N_TP
        down_kernel(*refs[:head], *refs[head + len(after) :])

    return pl.pallas_call(
        kernel,
        grid_spec=pltpu.PrefetchScalarGridSpec(
            num_scalar_prefetch=1,
            grid=(steps,),
            in_specs=[whole] * N_TP + [own] + [other] * (N_TP - 1) + [ANY] * len(after),
            out_specs=pl.BlockSpec((rows, piece), lambda i, m: (0, i)),
            scratch_shapes=[pltpu.VMEM((rows, hidden), BF16)] * N_TP,
        ),
        out_shape=pltpu.HBM((rows, part), BF16),
        compiler_params=BIG,
        cost_estimate=pl.CostEstimate(
            flops=8 * rows * hidden * part,
            bytes_accessed=8 * rows * hidden + 8 * hidden * part + 2 * rows * part,
            transcendentals=0,
        ),
        name="down_project",
    )(me, *packed, w_down, *moved, *after)


def mix_kernel(total_ref, hi_ref, lo_ref, back_ref, out_ref):
    back = back_ref[...]
    total = total_ref[...].astype(F32)
    for weight in (hi_ref, lo_ref):
        total = total + dot(weight[...], back)
    out_ref[...] = total.astype(out_ref.dtype)


def mix_in(total, hi, lo, back, dtype):
    rows, part = total.shape
    steps = 2
    column = pl.BlockSpec((rows, part // steps), lambda i: (0, i))
    weight = pl.BlockSpec(hi.shape, lambda i: (0, 0))
    return pl.pallas_call(
        mix_kernel,
        grid=(steps,),
        in_specs=[column, weight, weight,
                  pl.BlockSpec((back.shape[0], part // steps), lambda i: (0, i))],
        out_specs=column,
        out_shape=jax.ShapeDtypeStruct((rows, part), dtype),
        compiler_params=BIG,
        cost_estimate=pl.CostEstimate(
            flops=4 * hi.size * part, bytes_accessed=2 * back.size, transcendentals=0
        ),
        name="mix_in",
    )(total, hi, lo, back)


def body(
    queries, new_key, new_value, key_cache, value_cache, cache_len, residual,
    norm_gain, expert_ids, gate_probs, w_gate, w_up, w_down,
):
    rows, part = residual.shape
    group = ("side", "grp")
    devices = lax.axis_size("side") * lax.axis_size("grp")
    slots = devices * SLOTS
    me = lax.axis_index("tp").astype(jnp.int32).reshape(1)
    hi0, hi1, lo0, lo1, table0, table1 = route(expert_ids.T, gate_probs.T, devices)
    blocks = split_columns(me, w_down)
    gain = norm_gain.reshape(1, -1)
    inv_gain = 1.0 / gain
    summed, scaled = attention(
        cache_len, me, queries, new_key, new_value, key_cache, value_cache, residual, gain
    )
    swap = functools.partial(
        lax.all_to_all, axis_name=group, split_axis=0, concat_axis=0, tiled=True
    )
    moved = [exchange(*blocks[: N_TP - 1]), exchange(*blocks[N_TP - 1 :])]
    moved[0] = in_hbm(*moved[0])
    w_gate, w_up = in_hbm(w_gate, w_up)
    total = summed
    own = ()
    for expert, table, hi, lo in ((0, table0, hi0, lo0), (1, table1, hi1, lo1)):
        placed = place_rows(table, scaled)
        arrived = swap(placed.reshape(devices, SLOTS, part)).reshape(devices, 1, SLOTS, part)
        own = pick(arrived, 0, PICK_WEIGHT[expert], *moved[0], *moved[1])
        left = [lax.ppermute(half, "tp", RIGHT) for half in own]
        right = [lax.ppermute(half, "tp", LEFT) for half in own]
        low = lax.ppermute(left[0], "tp", RIGHT)
        high = lax.ppermute(right[1], "tp", LEFT)
        sums = near_project(me, (*own, *left, *right), w_gate, w_up, inv_gain, expert)
        packed = far_project(
            me, low, high, sums, w_gate, w_up, inv_gain, expert, FAR_WEIGHT[expert]
        )
        packed = packed, *exchange(packed, packed, packed)
        produced = down_project(me, packed, w_down, moved[expert], slots, expert)
        back = swap(produced.reshape(devices, SLOTS, part)).reshape(slots, part)
        total = mix_in(total, hi.T, lo.T, back, F32 if expert == 0 else BF16)
    return total


def solution(mesh):
    in_specs = (
        P(("side", "grp"), "tp"),
        P(("side", "grp"), "tp"),
        P(("side", "grp"), "tp"),
        P(("side", "grp"), None, "tp"),
        P(("side", "grp"), None, "tp"),
        P(("side", "grp")),
        P(("side", "grp"), "tp"),
        P(),
        P(("side", "grp"), None),
        P(("side", "grp"), None),
        P(("side", "grp"), "tp", None),
        P(("side", "grp"), "tp", None),
        P(("side", "grp"), "tp", None),
    )
    out_specs = P(("side", "grp"), "tp")
    return jax.shard_map(body, mesh=mesh, in_specs=in_specs, out_specs=out_specs, check_vma=False)
```

```python
import functools
import math

import jax
import jax.numpy as jnp
from jax import lax
from jax.experimental import pallas as pl
from jax.experimental.pallas import tpu as pltpu
from jax.sharding import PartitionSpec as P

HD = 128
TOPK = 8
EXP_DEV = 2
N_TP = 4
SLOTS = 8

epsilon = 1e-06
PICK_WEIGHT = (20, 0)
FAR_WEIGHT = (1, 14)
F32 = jnp.float32
BF16 = jnp.bfloat16


RIGHT = [(i, (i + 1) % N_TP) for i in range(N_TP)]
LEFT = [(i, (i - 1) % N_TP) for i in range(N_TP)]
ACROSS = [(i, (i + 2) % N_TP) for i in range(N_TP)]
VMEM = pl.BlockSpec(memory_space=pltpu.VMEM)
ANY = pl.BlockSpec(memory_space=pl.ANY)
BIG = pltpu.CompilerParams(vmem_limit_bytes=20 << 20)
dot = functools.partial(jnp.dot, preferred_element_type=F32)


def spread_of(slots, experts, j):
    owner = lax.broadcasted_iota(jnp.int32, (slots, experts), 0) // SLOTS
    expert = lax.broadcasted_iota(jnp.int32, (slots, experts), 1)
    return jnp.where(expert == owner * EXP_DEV + j, 1.0, 0.0).astype(BF16)


def chosen_of(spread, hits, earlier):
    shape = (spread.shape[0], hits.shape[1])
    slot = (lax.broadcasted_iota(jnp.int32, shape, 0) % SLOTS).astype(F32)
    return (dot(spread, hits) > 0.5) & (dot(spread, earlier) == slot)


def route_kernel(ids_ref, place_ref, hits_ref, earlier_ref):
    slots, rows = place_ref.shape
    experts = hits_ref.shape[0]
    ids = ids_ref[...]
    line = lax.broadcasted_iota(jnp.int32, (experts, rows), 0)
    hits = jnp.zeros((experts, rows), F32)
    for k in range(TOPK):
        hits = hits + jnp.where(ids[k : k + 1, :] == line, 1.0, 0.0)
    before = lax.broadcasted_iota(jnp.int32, (rows, rows), 0) < lax.broadcasted_iota(
        jnp.int32, (rows, rows), 1
    )
    hits = hits.astype(BF16)
    earlier = dot(hits, jnp.where(before, 1.0, 0.0).astype(BF16)).astype(BF16)
    hits_ref[...], earlier_ref[...] = hits, earlier
    chosen = chosen_of(spread_of(slots, experts, 0), hits, earlier)
    place_ref[...] = jnp.where(chosen, 1.0, 0.0).astype(BF16)


def weigh_kernel(ids_ref, probs_ref, hits_ref, earlier_ref, place_ref, *tables):
    slots, rows = place_ref.shape
    ids, probs = ids_ref[...], probs_ref[...]
    hits, earlier = hits_ref[...], earlier_ref[...]
    mix = probs / jnp.sum(probs, axis=0, keepdims=True)
    line = lax.broadcasted_iota(jnp.int32, hits.shape, 0)
    mixed = jnp.zeros(hits.shape, F32)
    for k in range(TOPK):
        mixed = mixed + jnp.where(ids[k : k + 1, :] == line, mix[k : k + 1, :], 0.0)
    mix_hi = mixed.astype(BF16)
    mix_lo = (mixed - mix_hi.astype(F32)).astype(BF16)
    for j in range(EXP_DEV):
        spread = spread_of(slots, hits.shape[0], j)
        chosen = chosen_of(spread, hits, earlier)
        tables[j][...] = jnp.where(chosen, dot(spread, mix_hi), 0.0).astype(BF16)
        tables[2 + j][...] = jnp.where(chosen, dot(spread, mix_lo), 0.0).astype(BF16)
        if j == 1:
            place_ref[...] = jnp.where(chosen, 1.0, 0.0).astype(BF16)


def route(ids, probs, devices):
    rows = ids.shape[1]
    table = jax.ShapeDtypeStruct((devices * SLOTS, rows), BF16)
    count = jax.ShapeDtypeStruct((devices * EXP_DEV, rows), BF16)
    place0, hits, earlier = pl.pallas_call(
        route_kernel,
        in_specs=[VMEM],
        out_specs=[VMEM] * 3,
        out_shape=[table, count, count],
        name="route",
    )(ids)
    place1, hi0, hi1, lo0, lo1 = pl.pallas_call(
        weigh_kernel,
        in_specs=[VMEM] * 4,
        out_specs=[VMEM] * 5,
        out_shape=[table] * 5,
        name="weigh",
    )(ids, probs, hits, earlier)
    return hi0, hi1, lo0, lo1, place0, place1


def split_columns(me, w):
    count, hidden, width = w.shape
    part = width // N_TP
    block = pl.BlockSpec((count, hidden // 2, part), lambda h, m: (0, h, 0))

    def kernel(me_ref, w_ref, *out_refs):
        for turn, out_ref in enumerate(out_refs):
            out_ref[...] = w_ref[:, :, columns(me_ref, turn + 1, part)]

    return pl.pallas_call(
        kernel,
        grid_spec=pltpu.PrefetchScalarGridSpec(
            num_scalar_prefetch=1,
            grid=(2,),
            in_specs=[pl.BlockSpec((count, hidden // 2, width), lambda h, m: (0, h, 0))],
            out_specs=[block] * (N_TP - 1),
        ),
        out_shape=[jax.ShapeDtypeStruct((count, hidden, part), w.dtype)] * (N_TP - 1),
        compiler_params=BIG,
        cost_estimate=pl.CostEstimate(flops=0, bytes_accessed=4 * w.size, transcendentals=0),
        name="split_columns",
    )(me, w)


def attention_kernel(
    lens_ref, q_ref, nk_ref, nv_ref, k_ref, v_ref, res_ref, gain_ref, summed_ref, scaled_ref
):
    rows, span, depth = k_ref.shape
    heads = q_ref.shape[1] // depth
    base = pl.program_id(0) * rows
    lines = rows * heads
    q = q_ref[...].astype(F32).reshape(rows, heads, depth)
    qb = q.astype(BF16)
    dims = (((1,), (1,)), ((), ()))
    scores = jnp.concatenate(
        [
            lax.dot_general(qb[r], k_ref[r], dims, preferred_element_type=F32)
            for r in range(rows)
        ],
        axis=0,
    )
    scale = 1.0 / math.sqrt(depth)
    line = lax.broadcasted_iota(jnp.int32, (lines, span), 0) // heads
    limit = jnp.zeros((lines, span), jnp.int32)
    for r in range(rows):
        limit = jnp.where(line == r, lens_ref[base + r], limit)
    live = lax.broadcasted_iota(jnp.int32, (lines, span), 1) < limit
    scores = jnp.where(live, scores * scale, -jnp.inf)
    fresh_key = jnp.broadcast_to(nk_ref[...].astype(F32)[:, None, :], (rows, heads, depth))
    fresh = jnp.sum(q * fresh_key, axis=2, keepdims=True).reshape(lines, 1) * scale
    top = jnp.maximum(jnp.max(scores, axis=1, keepdims=True), fresh)
    exps = jnp.exp(scores - top)
    fresh_exp = jnp.exp(fresh - top)
    total = jnp.sum(exps, axis=1, keepdims=True) + fresh_exp
    weights = (exps / total).astype(BF16)
    fresh_weight = (fresh_exp / total).astype(BF16).astype(F32)
    fresh_value = jnp.broadcast_to(nv_ref[...].astype(F32)[:, None, :], (rows, heads, depth))
    out = jnp.concatenate(
        [dot(weights[r * heads : (r + 1) * heads], v_ref[r]) for r in range(rows)], axis=0
    )
    out = out + fresh_weight * fresh_value.reshape(lines, depth)
    summed = res_ref[...].astype(F32) + out.reshape(rows, heads, depth).reshape(
        rows, heads * depth
    )
    summed_ref[...] = summed
    scaled_ref[...] = (summed * gain_ref[...]).astype(BF16)


def attention(lens, me, queries, new_key, new_value, keys, values, residual, gain):
    rows, part = queries.shape
    span, depth = keys.shape[1:]
    step = 32
    wide = pl.BlockSpec((step, part), lambda i, n, m: (i, 0))
    slim = pl.BlockSpec((step, depth), lambda i, n, m: (i, 0))
    cache = pl.BlockSpec((step, span, depth), lambda i, n, m: (i, 0, 0))

    def kernel(lens_ref, me_ref, *refs):
        attention_kernel(lens_ref, *refs)

    return pl.pallas_call(
        kernel,
        grid_spec=pltpu.PrefetchScalarGridSpec(
            num_scalar_prefetch=2,
            grid=(rows // step,),
            in_specs=[wide, slim, slim, cache, cache, wide,
                      pl.BlockSpec((1, part), lambda i, n, m: (0, m[0]))],
            out_specs=[wide, wide],
        ),
        out_shape=[
            jax.ShapeDtypeStruct((rows, part), F32), jax.ShapeDtypeStruct((rows, part), BF16)
        ],
        compiler_params=pltpu.CompilerParams(vmem_limit_bytes=58 << 20),
        cost_estimate=pl.CostEstimate(
            flops=4 * rows * part * span,
            bytes_accessed=4 * rows * span * depth,
            transcendentals=rows * part,
        ),
        name="attention",
    )(lens, me, queries, new_key, new_value, keys, values, residual, gain)


def place_kernel(table_ref, rows_ref, *refs):
    refs[-1][...] = dot(table_ref[...], rows_ref[...]).astype(BF16)


def place_rows(table, rows, *after):
    slots, part = table.shape[0], rows.shape[1]
    return pl.pallas_call(
        place_kernel,
        grid=(2,),
        in_specs=[
            pl.BlockSpec((slots // 2, table.shape[1]), lambda i: (i, 0)),
            pl.BlockSpec(rows.shape, lambda i: (0, 0)),
        ]
        + [ANY] * len(after),
        out_specs=pl.BlockSpec((slots // 2, part), lambda i: (i, 0)),
        out_shape=jax.ShapeDtypeStruct((slots, part), BF16),
        cost_estimate=pl.CostEstimate(
            flops=2 * table.size * part, bytes_accessed=4 * slots * part, transcendentals=0
        ),
        name="place_rows",
    )(table, rows, *after)


def pick_kernel(all_ref, *refs):
    for i, out_ref in enumerate(refs[-2:]):
        count = all_ref.shape[0] // 2
        out_ref[...] = all_ref[pl.ds(i * count, count)].reshape(out_ref.shape)


def pick(everything, expert, work, *after):
    devices, _, slots, part = everything.shape
    half = devices * slots // 2
    return pl.pallas_call(
        pick_kernel,
        grid=(1,),
        in_specs=[pl.BlockSpec((devices, 1, slots, part), lambda i: (0, expert, 0, 0))]
        + [ANY] * len(after),
        out_specs=[pl.BlockSpec((half, part), lambda i: (0, 0))] * 2,
        out_shape=[jax.ShapeDtypeStruct((half, part), everything.dtype)] * 2,
        compiler_params=BIG,
        cost_estimate=pl.CostEstimate(
            flops=int(work * 1e9), bytes_accessed=8 * half * part, transcendentals=0
        ),
        name="pick",
    )(everything, *after)


def in_hbm(*arrays):
    return [pltpu.with_memory_space_constraint(array, pltpu.HBM) for array in arrays]


def exchange(for_right, for_across, for_left):
    return (
        lax.ppermute(for_right, "tp", RIGHT),
        lax.ppermute(for_left, "tp", LEFT),
        lax.ppermute(for_across, "tp", ACROSS),
    )


def columns(me_ref, turn, part):
    return pl.ds(pl.multiple_of(lax.rem(me_ref[0] + turn, N_TP) * part, part), part)


def project(x, cols, gate_ref, up_ref, inv_ref):
    dims = (((1,), (1,)), ((), ()))
    plain = x.astype(F32) * inv_ref[:, cols]
    return (
        lax.dot_general(x, gate_ref[0, :, cols], dims, preferred_element_type=F32),
        lax.dot_general(x, up_ref[0, :, cols], dims, preferred_element_type=F32),
        jnp.sum(plain * plain, axis=1, keepdims=True),
    )


def near_kernel(
    me_ref, own0, own1, left0, left1, right0, right1, gate_ref, up_ref, inv_ref,
    gate_out, up_out, sq_out,
):
    half, part = own0.shape
    for i, blocks in enumerate(((own0, left0, right0), (own1, left1, right1))):
        rows = pl.ds(i * half, half)
        total = None
        for block, turn in zip(blocks, (0, N_TP - 1, 1), strict=True):
            term = project(block[...], columns(me_ref, turn, part), gate_ref, up_ref, inv_ref)
            total = term if total is None else tuple(
                a + b for a, b in zip(total, term, strict=True)
            )
        gate_out[rows, :], up_out[rows, :] = total[0], total[1]
        sq_out[rows, :] = jnp.broadcast_to(total[2], (half, sq_out.shape[1]))


def far_kernel(me_ref, low, high, gate_in, up_in, sq_in, gate_ref, up_ref, inv_ref, out_ref):
    half, part = low.shape
    hidden = gate_in.shape[1]
    tails = []
    for i, block in enumerate((low, high)):
        rows = slice(i * half, (i + 1) * half)
        cols = pl.ds(0, part)
        gate, up, squares = project(block[...], cols, gate_ref, up_ref, inv_ref)
        scale = lax.rsqrt((sq_in[rows, :1] + squares) / (N_TP * part) + epsilon)
        gate, up = (gate_in[rows] + gate) * scale, (up_in[rows] + up) * scale
        value = gate / (1.0 + jnp.exp(-gate)) * up
        out_ref[rows, :] = value[:, :128].astype(BF16)
        tails.append(value[:, 128:hidden])
    out_ref[2 * half :, :] = jnp.concatenate(tails, axis=1).astype(BF16)


def near_project(me, blocks, w_gate, w_up, inv_gain, expert):
    rows, part = 2 * blocks[0].shape[0], blocks[0].shape[1]
    hidden, width = w_gate.shape[1:]

    def whole(shape):
        return pl.BlockSpec(shape, lambda i, m: (0,) * len(shape))

    weight = pl.BlockSpec((1, hidden, width), lambda i, m: (expert, 0, 0))
    return pl.pallas_call(
        near_kernel,
        grid_spec=pltpu.PrefetchScalarGridSpec(
            num_scalar_prefetch=1,
            grid=(1,),
            in_specs=[whole(blocks[0].shape)] * 6 + [weight, weight, whole((1, width))],
            out_specs=[whole((rows, hidden)), whole((rows, hidden)), whole((rows, 128))],
        ),
        out_shape=[jax.ShapeDtypeStruct((rows, hidden), F32)] * 2
        + [jax.ShapeDtypeStruct((rows, 128), F32)],
        compiler_params=pltpu.CompilerParams(vmem_limit_bytes=32 << 20),
        cost_estimate=pl.CostEstimate(
            flops=3 * rows * width * hidden,
            bytes_accessed=2 * rows * width + 4 * hidden * width,
            transcendentals=0,
        ),
        name="near_project",
    )(me, *blocks, w_gate, w_up, inv_gain)


def far_project(me, low, high, near, w_gate, w_up, inv_gain, expert, weight_us):
    half, part = low.shape
    hidden, width = w_gate.shape[1:]
    rows = 2 * half

    def whole(shape):
        return pl.BlockSpec(shape, lambda i, m: (0,) * len(shape))

    def across(m):
        return lax.rem(m[0] + 2, N_TP)

    weight = pl.BlockSpec((1, hidden, part), lambda i, m: (expert, 0, across(m)))
    packed = (rows + rows * (hidden - 128) // 128, 128)

    return pl.pallas_call(
        far_kernel,
        grid_spec=pltpu.PrefetchScalarGridSpec(
            num_scalar_prefetch=1,
            grid=(1,),
            in_specs=[whole(low.shape), whole(high.shape)]
            + [whole(a.shape) for a in near]
            + [weight, weight, pl.BlockSpec((1, part), lambda i, m: (0, across(m)))],
            out_specs=whole(packed),
        ),
        out_shape=jax.ShapeDtypeStruct(packed, BF16),
        compiler_params=BIG,
        cost_estimate=pl.CostEstimate(
            flops=int(weight_us * 1e9), bytes_accessed=8 * rows * part, transcendentals=0
        ),
        name="far_project",
    )(me, low, high, *near, w_gate, w_up, inv_gain)


def down_kernel(me_ref, h0, h1, h2, h3, w0, w1, w2, w3, out_ref, *plain):
    rows, hidden = plain[0].shape

    @pl.when(pl.program_id(0) == 0)
    def _():
        for packed, full in zip((h0, h1, h2, h3), plain, strict=True):
            tails = packed[rows:, :]
            full[:, :128] = packed[:rows, :]
            full[: rows // 2, 128:] = tails[:, : hidden - 128]
            full[rows // 2 :, 128:] = tails[:, hidden - 128 :]

    total = None
    for full, w_ref in zip(plain, (w0, w1, w2, w3), strict=True):
        term = dot(full[...], w_ref[0])
        total = term if total is None else total + term
    out_ref[...] = total.astype(out_ref.dtype)


def down_project(me, packed, w_down, moved, rows, expert, *after):
    _, hidden, part = moved[0].shape
    whole = pl.BlockSpec(packed[0].shape, lambda i, m: (0, 0))
    steps = 2
    piece = part // steps
    own = pl.BlockSpec((1, hidden, piece), lambda i, m: (expert, 0, m[0] * steps + i))
    other = pl.BlockSpec((1, hidden, piece), lambda i, m: (expert, 0, i))

    def kernel(*refs):
        head = 1 + 2 * N_TP
        down_kernel(*refs[:head], *refs[head + len(after) :])

    return pl.pallas_call(
        kernel,
        grid_spec=pltpu.PrefetchScalarGridSpec(
            num_scalar_prefetch=1,
            grid=(steps,),
            in_specs=[whole] * N_TP + [own] + [other] * (N_TP - 1) + [ANY] * len(after),
            out_specs=pl.BlockSpec((rows, piece), lambda i, m: (0, i)),
            scratch_shapes=[pltpu.VMEM((rows, hidden), BF16)] * N_TP,
        ),
        out_shape=pltpu.HBM((rows, part), BF16),
        compiler_params=BIG,
        cost_estimate=pl.CostEstimate(
            flops=8 * rows * hidden * part,
            bytes_accessed=8 * rows * hidden + 8 * hidden * part + 2 * rows * part,
            transcendentals=0,
        ),
        name="down_project",
    )(me, *packed, w_down, *moved, *after)


def mix_kernel(total_ref, hi_ref, lo_ref, back_ref, out_ref):
    back = back_ref[...]
    total = total_ref[...].astype(F32)
    for weight in (hi_ref, lo_ref):
        total = total + dot(weight[...], back)
    out_ref[...] = total.astype(out_ref.dtype)


def mix_in(total, hi, lo, back, dtype):
    rows, part = total.shape
    steps = 2
    column = pl.BlockSpec((rows, part // steps), lambda i: (0, i))
    weight = pl.BlockSpec(hi.shape, lambda i: (0, 0))
    return pl.pallas_call(
        mix_kernel,
        grid=(steps,),
        in_specs=[column, weight, weight,
                  pl.BlockSpec((back.shape[0], part // steps), lambda i: (0, i))],
        out_specs=column,
        out_shape=jax.ShapeDtypeStruct((rows, part), dtype),
        compiler_params=BIG,
        cost_estimate=pl.CostEstimate(
            flops=4 * hi.size * part, bytes_accessed=2 * back.size, transcendentals=0
        ),
        name="mix_in",
    )(total, hi, lo, back)


def body(
    queries, new_key, new_value, key_cache, value_cache, cache_len, residual,
    norm_gain, expert_ids, gate_probs, w_gate, w_up, w_down,
):
    rows, part = residual.shape
    group = ("side", "grp")
    devices = lax.axis_size("side") * lax.axis_size("grp")
    slots = devices * SLOTS
    me = lax.axis_index("tp").astype(jnp.int32).reshape(1)
    hi0, hi1, lo0, lo1, table0, table1 = route(expert_ids.T, gate_probs.T, devices)
    blocks = split_columns(me, w_down)
    gain = norm_gain.reshape(1, -1)
    inv_gain = 1.0 / gain
    summed, scaled = attention(
        cache_len, me, queries, new_key, new_value, key_cache, value_cache, residual, gain
    )
    swap = functools.partial(
        lax.all_to_all, axis_name=group, split_axis=0, concat_axis=0, tiled=True
    )
    moved = in_hbm(*exchange(*blocks))
    w_gate, w_up = in_hbm(w_gate, w_up)
    total = summed
    own = ()
    for expert, table, hi, lo in ((0, table0, hi0, lo0), (1, table1, hi1, lo1)):
        placed = place_rows(table, scaled)
        arrived = swap(placed.reshape(devices, SLOTS, part)).reshape(devices, 1, SLOTS, part)
        own = pick(arrived, 0, PICK_WEIGHT[expert], *moved[: 3 * expert])
        left = [lax.ppermute(half, "tp", RIGHT) for half in own]
        right = [lax.ppermute(half, "tp", LEFT) for half in own]
        low = lax.ppermute(left[0], "tp", RIGHT)
        high = lax.ppermute(right[1], "tp", LEFT)
        sums = near_project(me, (*own, *left, *right), w_gate, w_up, inv_gain, expert)
        packed = far_project(
            me, low, high, sums, w_gate, w_up, inv_gain, expert, FAR_WEIGHT[expert]
        )
        packed = packed, *exchange(packed, packed, packed)
        produced = down_project(me, packed, w_down, moved, slots, expert)
        back = swap(produced.reshape(devices, SLOTS, part)).reshape(slots, part)
        total = mix_in(total, hi.T, lo.T, back, F32 if expert == 0 else BF16)
    return total


def solution(mesh):
    in_specs = (
        P(("side", "grp"), "tp"),
        P(("side", "grp"), "tp"),
        P(("side", "grp"), "tp"),
        P(("side", "grp"), None, "tp"),
        P(("side", "grp"), None, "tp"),
        P(("side", "grp")),
        P(("side", "grp"), "tp"),
        P(),
        P(("side", "grp"), None),
        P(("side", "grp"), None),
        P(("side", "grp"), "tp", None),
        P(("side", "grp"), "tp", None),
        P(("side", "grp"), "tp", None),
    )
    out_specs = P(("side", "grp"), "tp")
    return jax.shard_map(body, mesh=mesh, in_specs=in_specs, out_specs=out_specs, check_vma=False)
```

```python
import functools
import math

import jax
import jax.numpy as jnp
from jax import lax
from jax.experimental import pallas as pl
from jax.experimental.pallas import tpu as pltpu
from jax.sharding import PartitionSpec as P

HD = 128
TOPK = 8
EXP_DEV = 2
N_TP = 4
SLOTS = 8

epsilon = 1e-06
PICK_WEIGHT = (20, 0)
FAR_WEIGHT = (1, 14)
F32 = jnp.float32
BF16 = jnp.bfloat16


RIGHT = [(i, (i + 1) % N_TP) for i in range(N_TP)]
LEFT = [(i, (i - 1) % N_TP) for i in range(N_TP)]
ACROSS = [(i, (i + 2) % N_TP) for i in range(N_TP)]
VMEM = pl.BlockSpec(memory_space=pltpu.VMEM)
ANY = pl.BlockSpec(memory_space=pl.ANY)
BIG = pltpu.CompilerParams(vmem_limit_bytes=20 << 20)
dot = functools.partial(jnp.dot, preferred_element_type=F32)


def spread_of(slots, experts, j):
    owner = lax.broadcasted_iota(jnp.int32, (slots, experts), 0) // SLOTS
    expert = lax.broadcasted_iota(jnp.int32, (slots, experts), 1)
    return jnp.where(expert == owner * EXP_DEV + j, 1.0, 0.0).astype(BF16)


def chosen_of(spread, hits, earlier):
    shape = (spread.shape[0], hits.shape[1])
    slot = (lax.broadcasted_iota(jnp.int32, shape, 0) % SLOTS).astype(F32)
    return (dot(spread, hits) > 0.5) & (dot(spread, earlier) == slot)


def counts_of(ids, experts):
    rows = ids.shape[1]
    line = lax.broadcasted_iota(jnp.int32, (experts, rows), 0)
    hits = jnp.zeros((experts, rows), F32)
    for k in range(TOPK):
        hits = hits + jnp.where(ids[k : k + 1, :] == line, 1.0, 0.0)
    before = lax.broadcasted_iota(jnp.int32, (rows, rows), 0) < lax.broadcasted_iota(
        jnp.int32, (rows, rows), 1
    )
    hits = hits.astype(BF16)
    return hits, dot(hits, jnp.where(before, 1.0, 0.0).astype(BF16)).astype(BF16)


def weigh_kernel(ids_ref, probs_ref, place_ref, *tables):
    slots, rows = place_ref.shape
    experts = EXP_DEV * slots // SLOTS
    ids, probs = ids_ref[...], probs_ref[...]
    hits, earlier = counts_of(ids, experts)
    mix = probs / jnp.sum(probs, axis=0, keepdims=True)
    line = lax.broadcasted_iota(jnp.int32, hits.shape, 0)
    mixed = jnp.zeros(hits.shape, F32)
    for k in range(TOPK):
        mixed = mixed + jnp.where(ids[k : k + 1, :] == line, mix[k : k + 1, :], 0.0)
    mix_hi = mixed.astype(BF16)
    mix_lo = (mixed - mix_hi.astype(F32)).astype(BF16)
    for j in range(EXP_DEV):
        spread = spread_of(slots, experts, j)
        chosen = chosen_of(spread, hits, earlier)
        tables[j][...] = jnp.where(chosen, dot(spread, mix_hi), 0.0).astype(BF16)
        tables[2 + j][...] = jnp.where(chosen, dot(spread, mix_lo), 0.0).astype(BF16)
        if j == 1:
            place_ref[...] = jnp.where(chosen, 1.0, 0.0).astype(BF16)


def weigh(ids, probs, devices, after):
    table = jax.ShapeDtypeStruct((devices * SLOTS, ids.shape[1]), BF16)

    def kernel(ids_ref, probs_ref, _, *tables):
        weigh_kernel(ids_ref, probs_ref, *tables)

    return pl.pallas_call(
        kernel,
        in_specs=[VMEM, VMEM, ANY],
        out_specs=[VMEM] * 5,
        out_shape=[table] * 5,
        name="weigh",
    )(ids, probs, after)


def split_columns(me, w):
    count, hidden, width = w.shape
    part = width // N_TP
    block = pl.BlockSpec((count, hidden // 2, part), lambda h, m: (0, h, 0))

    def kernel(me_ref, w_ref, *out_refs):
        for turn, out_ref in enumerate(out_refs):
            out_ref[...] = w_ref[:, :, columns(me_ref, turn + 1, part)]

    return pl.pallas_call(
        kernel,
        grid_spec=pltpu.PrefetchScalarGridSpec(
            num_scalar_prefetch=1,
            grid=(2,),
            in_specs=[pl.BlockSpec((count, hidden // 2, width), lambda h, m: (0, h, 0))],
            out_specs=[block] * (N_TP - 1),
        ),
        out_shape=[jax.ShapeDtypeStruct((count, hidden, part), w.dtype)] * (N_TP - 1),
        compiler_params=BIG,
        cost_estimate=pl.CostEstimate(flops=0, bytes_accessed=4 * w.size, transcendentals=0),
        name="split_columns",
    )(me, w)


def attention_kernel(
    lens_ref, q_ref, nk_ref, nv_ref, k_ref, v_ref, res_ref, gain_ref, ids_ref,
    summed_ref, scaled_ref, placed_ref, table, held
):
    rows, span, depth = k_ref.shape
    heads = q_ref.shape[1] // depth
    base = pl.program_id(0) * rows
    lines = rows * heads
    q = q_ref[...].astype(F32).reshape(rows, heads, depth)
    qb = q.astype(BF16)
    dims = (((1,), (1,)), ((), ()))
    scores = jnp.concatenate(
        [
            lax.dot_general(qb[r], k_ref[r], dims, preferred_element_type=F32)
            for r in range(rows)
        ],
        axis=0,
    )
    scale = 1.0 / math.sqrt(depth)
    line = lax.broadcasted_iota(jnp.int32, (lines, span), 0) // heads
    limit = jnp.zeros((lines, span), jnp.int32)
    for r in range(rows):
        limit = jnp.where(line == r, lens_ref[base + r], limit)
    live = lax.broadcasted_iota(jnp.int32, (lines, span), 1) < limit
    scores = jnp.where(live, scores * scale, -jnp.inf)
    fresh_key = jnp.broadcast_to(nk_ref[...].astype(F32)[:, None, :], (rows, heads, depth))
    fresh = jnp.sum(q * fresh_key, axis=2, keepdims=True).reshape(lines, 1) * scale
    top = jnp.maximum(jnp.max(scores, axis=1, keepdims=True), fresh)
    exps = jnp.exp(scores - top)
    fresh_exp = jnp.exp(fresh - top)
    total = jnp.sum(exps, axis=1, keepdims=True) + fresh_exp
    weights = (exps / total).astype(BF16)
    fresh_weight = (fresh_exp / total).astype(BF16).astype(F32)
    fresh_value = jnp.broadcast_to(nv_ref[...].astype(F32)[:, None, :], (rows, heads, depth))
    out = jnp.concatenate(
        [dot(weights[r * heads : (r + 1) * heads], v_ref[r]) for r in range(rows)], axis=0
    )
    out = out + fresh_weight * fresh_value.reshape(lines, depth)
    summed = res_ref[...].astype(F32) + out.reshape(rows, heads, depth).reshape(
        rows, heads * depth
    )
    summed_ref[...] = summed
    scaled = (summed * gain_ref[...]).astype(BF16)
    scaled_ref[...] = scaled
    held[pl.ds(pl.multiple_of(base, rows), rows), :] = scaled

    @pl.when(pl.program_id(0) == 0)
    def _():
        slots = table.shape[0]
        experts = EXP_DEV * slots // SLOTS
        hits, earlier = counts_of(ids_ref[...], experts)
        chosen = chosen_of(spread_of(slots, experts, 0), hits, earlier)
        table[...] = jnp.where(chosen, 1.0, 0.0).astype(BF16)

    @pl.when(pl.program_id(0) == pl.num_programs(0) - 1)
    def _():
        placed_ref[...] = dot(table[...], held[...]).astype(BF16)


def attention(lens, me, queries, new_key, new_value, keys, values, residual, gain, ids, devices):
    rows, part = queries.shape
    span, depth = keys.shape[1:]
    step = 32
    wide = pl.BlockSpec((step, part), lambda i, n, m: (i, 0))
    slim = pl.BlockSpec((step, depth), lambda i, n, m: (i, 0))
    cache = pl.BlockSpec((step, span, depth), lambda i, n, m: (i, 0, 0))

    def kernel(lens_ref, me_ref, *refs):
        attention_kernel(lens_ref, *refs)

    return pl.pallas_call(
        kernel,
        grid_spec=pltpu.PrefetchScalarGridSpec(
            num_scalar_prefetch=2,
            grid=(rows // step,),
            in_specs=[wide, slim, slim, cache, cache, wide,
                      pl.BlockSpec((1, part), lambda i, n, m: (0, m[0])),
                      pl.BlockSpec(ids.shape, lambda i, n, m: (0, 0))],
            out_specs=[wide, wide,
                       pl.BlockSpec((devices * SLOTS, part), lambda i, n, m: (0, 0))],
            scratch_shapes=[
                pltpu.VMEM((devices * SLOTS, rows), BF16), pltpu.VMEM((rows, part), BF16)
            ],
        ),
        out_shape=[
            jax.ShapeDtypeStruct((rows, part), F32),
            jax.ShapeDtypeStruct((rows, part), BF16),
            jax.ShapeDtypeStruct((devices * SLOTS, part), BF16),
        ],
        compiler_params=pltpu.CompilerParams(vmem_limit_bytes=58 << 20),
        cost_estimate=pl.CostEstimate(
            flops=4 * rows * part * span,
            bytes_accessed=4 * rows * span * depth,
            transcendentals=rows * part,
        ),
        name="attention",
    )(lens, me, queries, new_key, new_value, keys, values, residual, gain, ids)


def place_kernel(table_ref, rows_ref, *refs):
    refs[-1][...] = dot(table_ref[...], rows_ref[...]).astype(BF16)


def place_rows(table, rows, *after):
    slots, part = table.shape[0], rows.shape[1]
    return pl.pallas_call(
        place_kernel,
        grid=(2,),
        in_specs=[
            pl.BlockSpec((slots // 2, table.shape[1]), lambda i: (i, 0)),
            pl.BlockSpec(rows.shape, lambda i: (0, 0)),
        ]
        + [ANY] * len(after),
        out_specs=pl.BlockSpec((slots // 2, part), lambda i: (i, 0)),
        out_shape=jax.ShapeDtypeStruct((slots, part), BF16),
        cost_estimate=pl.CostEstimate(
            flops=2 * table.size * part, bytes_accessed=4 * slots * part, transcendentals=0
        ),
        name="place_rows",
    )(table, rows, *after)


def pick_kernel(all_ref, *refs):
    for i, out_ref in enumerate(refs[-2:]):
        count = all_ref.shape[0] // 2
        out_ref[...] = all_ref[pl.ds(i * count, count)].reshape(out_ref.shape)


def pick(everything, expert, work, *after):
    devices, _, slots, part = everything.shape
    half = devices * slots // 2
    return pl.pallas_call(
        pick_kernel,
        grid=(1,),
        in_specs=[pl.BlockSpec((devices, 1, slots, part), lambda i: (0, expert, 0, 0))]
        + [ANY] * len(after),
        out_specs=[pl.BlockSpec((half, part), lambda i: (0, 0))] * 2,
        out_shape=[jax.ShapeDtypeStruct((half, part), everything.dtype)] * 2,
        compiler_params=BIG,
        cost_estimate=pl.CostEstimate(
            flops=int(work * 1e9), bytes_accessed=8 * half * part, transcendentals=0
        ),
        name="pick",
    )(everything, *after)


def in_hbm(*arrays):
    return [pltpu.with_memory_space_constraint(array, pltpu.HBM) for array in arrays]


def exchange(for_right, for_across, for_left):
    return (
        lax.ppermute(for_right, "tp", RIGHT),
        lax.ppermute(for_left, "tp", LEFT),
        lax.ppermute(for_across, "tp", ACROSS),
    )


def columns(me_ref, turn, part):
    return pl.ds(pl.multiple_of(lax.rem(me_ref[0] + turn, N_TP) * part, part), part)


def project(x, cols, gate_ref, up_ref, inv_ref):
    dims = (((1,), (1,)), ((), ()))
    plain = x.astype(F32) * inv_ref[:, cols]
    return (
        lax.dot_general(x, gate_ref[0, :, cols], dims, preferred_element_type=F32),
        lax.dot_general(x, up_ref[0, :, cols], dims, preferred_element_type=F32),
        jnp.sum(plain * plain, axis=1, keepdims=True),
    )


def near_kernel(
    me_ref, own0, own1, left0, left1, right0, right1, gate_ref, up_ref, inv_ref,
    gate_out, up_out, sq_out,
):
    half, part = own0.shape
    for i, blocks in enumerate(((own0, left0, right0), (own1, left1, right1))):
        rows = pl.ds(i * half, half)
        total = None
        for block, turn in zip(blocks, (0, N_TP - 1, 1), strict=True):
            term = project(block[...], columns(me_ref, turn, part), gate_ref, up_ref, inv_ref)
            total = term if total is None else tuple(
                a + b for a, b in zip(total, term, strict=True)
            )
        gate_out[rows, :], up_out[rows, :] = total[0], total[1]
        sq_out[rows, :] = jnp.broadcast_to(total[2], (half, sq_out.shape[1]))


def far_kernel(me_ref, low, high, gate_in, up_in, sq_in, gate_ref, up_ref, inv_ref, out_ref):
    half, part = low.shape
    hidden = gate_in.shape[1]
    tails = []
    for i, block in enumerate((low, high)):
        rows = slice(i * half, (i + 1) * half)
        cols = pl.ds(0, part)
        gate, up, squares = project(block[...], cols, gate_ref, up_ref, inv_ref)
        scale = lax.rsqrt((sq_in[rows, :1] + squares) / (N_TP * part) + epsilon)
        gate, up = (gate_in[rows] + gate) * scale, (up_in[rows] + up) * scale
        value = gate / (1.0 + jnp.exp(-gate)) * up
        out_ref[rows, :] = value[:, :128].astype(BF16)
        tails.append(value[:, 128:hidden])
    out_ref[2 * half :, :] = jnp.concatenate(tails, axis=1).astype(BF16)


def near_project(me, blocks, w_gate, w_up, inv_gain, expert):
    rows, part = 2 * blocks[0].shape[0], blocks[0].shape[1]
    hidden, width = w_gate.shape[1:]

    def whole(shape):
        return pl.BlockSpec(shape, lambda i, m: (0,) * len(shape))

    weight = pl.BlockSpec((1, hidden, width), lambda i, m: (expert, 0, 0))
    return pl.pallas_call(
        near_kernel,
        grid_spec=pltpu.PrefetchScalarGridSpec(
            num_scalar_prefetch=1,
            grid=(1,),
            in_specs=[whole(blocks[0].shape)] * 6 + [weight, weight, whole((1, width))],
            out_specs=[whole((rows, hidden)), whole((rows, hidden)), whole((rows, 128))],
        ),
        out_shape=[jax.ShapeDtypeStruct((rows, hidden), F32)] * 2
        + [jax.ShapeDtypeStruct((rows, 128), F32)],
        compiler_params=pltpu.CompilerParams(vmem_limit_bytes=32 << 20),
        cost_estimate=pl.CostEstimate(
            flops=3 * rows * width * hidden,
            bytes_accessed=2 * rows * width + 4 * hidden * width,
            transcendentals=0,
        ),
        name="near_project",
    )(me, *blocks, w_gate, w_up, inv_gain)


def far_project(me, low, high, near, w_gate, w_up, inv_gain, expert, weight_us):
    half, part = low.shape
    hidden, width = w_gate.shape[1:]
    rows = 2 * half

    def whole(shape):
        return pl.BlockSpec(shape, lambda i, m: (0,) * len(shape))

    def across(m):
        return lax.rem(m[0] + 2, N_TP)

    weight = pl.BlockSpec((1, hidden, part), lambda i, m: (expert, 0, across(m)))
    packed = (rows + rows * (hidden - 128) // 128, 128)

    return pl.pallas_call(
        far_kernel,
        grid_spec=pltpu.PrefetchScalarGridSpec(
            num_scalar_prefetch=1,
            grid=(1,),
            in_specs=[whole(low.shape), whole(high.shape)]
            + [whole(a.shape) for a in near]
            + [weight, weight, pl.BlockSpec((1, part), lambda i, m: (0, across(m)))],
            out_specs=whole(packed),
        ),
        out_shape=jax.ShapeDtypeStruct(packed, BF16),
        compiler_params=BIG,
        cost_estimate=pl.CostEstimate(
            flops=int(weight_us * 1e9), bytes_accessed=8 * rows * part, transcendentals=0
        ),
        name="far_project",
    )(me, low, high, *near, w_gate, w_up, inv_gain)


def down_kernel(me_ref, h0, h1, h2, h3, w0, w1, w2, w3, out_ref, *plain):
    rows, hidden = plain[0].shape

    @pl.when(pl.program_id(0) == 0)
    def _():
        for packed, full in zip((h0, h1, h2, h3), plain, strict=True):
            tails = packed[rows:, :]
            full[:, :128] = packed[:rows, :]
            full[: rows // 2, 128:] = tails[:, : hidden - 128]
            full[rows // 2 :, 128:] = tails[:, hidden - 128 :]

    total = None
    for full, w_ref in zip(plain, (w0, w1, w2, w3), strict=True):
        term = dot(full[...], w_ref[0])
        total = term if total is None else total + term
    out_ref[...] = total.astype(out_ref.dtype)


def down_project(me, packed, w_down, moved, rows, expert, *after):
    _, hidden, part = moved[0].shape
    whole = pl.BlockSpec(packed[0].shape, lambda i, m: (0, 0))
    steps = 2
    piece = part // steps
    own = pl.BlockSpec((1, hidden, piece), lambda i, m: (expert, 0, m[0] * steps + i))
    other = pl.BlockSpec((1, hidden, piece), lambda i, m: (expert, 0, i))

    def kernel(*refs):
        head = 1 + 2 * N_TP
        down_kernel(*refs[:head], *refs[head + len(after) :])

    return pl.pallas_call(
        kernel,
        grid_spec=pltpu.PrefetchScalarGridSpec(
            num_scalar_prefetch=1,
            grid=(steps,),
            in_specs=[whole] * N_TP + [own] + [other] * (N_TP - 1) + [ANY] * len(after),
            out_specs=pl.BlockSpec((rows, piece), lambda i, m: (0, i)),
            scratch_shapes=[pltpu.VMEM((rows, hidden), BF16)] * N_TP,
        ),
        out_shape=pltpu.HBM((rows, part), BF16),
        compiler_params=BIG,
        cost_estimate=pl.CostEstimate(
            flops=8 * rows * hidden * part,
            bytes_accessed=8 * rows * hidden + 8 * hidden * part + 2 * rows * part,
            transcendentals=0,
        ),
        name="down_project",
    )(me, *packed, w_down, *moved, *after)


def mix_kernel(total_ref, hi_ref, lo_ref, back_ref, out_ref):
    back = back_ref[...]
    total = total_ref[...].astype(F32)
    for weight in (hi_ref, lo_ref):
        total = total + dot(weight[...], back)
    out_ref[...] = total.astype(out_ref.dtype)


def mix_in(total, hi, lo, back, dtype):
    rows, part = total.shape
    steps = 2
    column = pl.BlockSpec((rows, part // steps), lambda i: (0, i))
    weight = pl.BlockSpec(hi.shape, lambda i: (0, 0))
    return pl.pallas_call(
        mix_kernel,
        grid=(steps,),
        in_specs=[column, weight, weight,
                  pl.BlockSpec((back.shape[0], part // steps), lambda i: (0, i))],
        out_specs=column,
        out_shape=jax.ShapeDtypeStruct((rows, part), dtype),
        compiler_params=BIG,
        cost_estimate=pl.CostEstimate(
            flops=4 * hi.size * part, bytes_accessed=2 * back.size, transcendentals=0
        ),
        name="mix_in",
    )(total, hi, lo, back)


def body(
    queries, new_key, new_value, key_cache, value_cache, cache_len, residual,
    norm_gain, expert_ids, gate_probs, w_gate, w_up, w_down,
):
    rows, part = residual.shape
    group = ("side", "grp")
    devices = lax.axis_size("side") * lax.axis_size("grp")
    slots = devices * SLOTS
    me = lax.axis_index("tp").astype(jnp.int32).reshape(1)
    blocks = split_columns(me, w_down)
    gain = norm_gain.reshape(1, -1)
    inv_gain = 1.0 / gain
    ids = expert_ids.T
    summed, scaled, placed0 = attention(
        cache_len, me, queries, new_key, new_value, key_cache, value_cache, residual, gain,
        ids, devices,
    )
    table1, hi0, hi1, lo0, lo1 = weigh(ids, gate_probs.T, devices, blocks[0])
    swap = functools.partial(
        lax.all_to_all, axis_name=group, split_axis=0, concat_axis=0, tiled=True
    )
    moved = in_hbm(*exchange(*blocks))
    w_gate, w_up = in_hbm(w_gate, w_up)
    total = summed
    own = ()
    for expert, hi, lo in ((0, hi0, lo0), (1, hi1, lo1)):
        placed = place_rows(table1, scaled) if expert else placed0
        arrived = swap(placed.reshape(devices, SLOTS, part)).reshape(devices, 1, SLOTS, part)
        own = pick(arrived, 0, PICK_WEIGHT[expert], *moved[: 3 * expert])
        left = [lax.ppermute(half, "tp", RIGHT) for half in own]
        right = [lax.ppermute(half, "tp", LEFT) for half in own]
        low = lax.ppermute(left[0], "tp", RIGHT)
        high = lax.ppermute(right[1], "tp", LEFT)
        sums = near_project(me, (*own, *left, *right), w_gate, w_up, inv_gain, expert)
        packed = far_project(
            me, low, high, sums, w_gate, w_up, inv_gain, expert, FAR_WEIGHT[expert]
        )
        packed = packed, *exchange(packed, packed, packed)
        produced = down_project(me, packed, w_down, moved, slots, expert)
        back = swap(produced.reshape(devices, SLOTS, part)).reshape(slots, part)
        total = mix_in(total, hi.T, lo.T, back, F32 if expert == 0 else BF16)
    return total


def solution(mesh):
    in_specs = (
        P(("side", "grp"), "tp"),
        P(("side", "grp"), "tp"),
        P(("side", "grp"), "tp"),
        P(("side", "grp"), None, "tp"),
        P(("side", "grp"), None, "tp"),
        P(("side", "grp")),
        P(("side", "grp"), "tp"),
        P(),
        P(("side", "grp"), None),
        P(("side", "grp"), None),
        P(("side", "grp"), "tp", None),
        P(("side", "grp"), "tp", None),
        P(("side", "grp"), "tp", None),
    )
    out_specs = P(("side", "grp"), "tp")
    return jax.shard_map(body, mesh=mesh, in_specs=in_specs, out_specs=out_specs, check_vma=False)
```

```python
import functools
import math

import jax
import jax.numpy as jnp
from jax import lax
from jax.experimental import pallas as pl
from jax.experimental.pallas import tpu as pltpu
from jax.sharding import PartitionSpec as P

HD = 128
TOPK = 8
EXP_DEV = 2
N_TP = 4
SLOTS = 8

epsilon = 1e-06
PICK_WEIGHT = (20, 0)
FAR_WEIGHT = (1, 14)
F32 = jnp.float32
BF16 = jnp.bfloat16


RIGHT = [(i, (i + 1) % N_TP) for i in range(N_TP)]
LEFT = [(i, (i - 1) % N_TP) for i in range(N_TP)]
ACROSS = [(i, (i + 2) % N_TP) for i in range(N_TP)]
VMEM = pl.BlockSpec(memory_space=pltpu.VMEM)
ANY = pl.BlockSpec(memory_space=pl.ANY)
BIG = pltpu.CompilerParams(vmem_limit_bytes=20 << 20)
dot = functools.partial(jnp.dot, preferred_element_type=F32)


def spread_of(slots, experts, j):
    owner = lax.broadcasted_iota(jnp.int32, (slots, experts), 0) // SLOTS
    expert = lax.broadcasted_iota(jnp.int32, (slots, experts), 1)
    return jnp.where(expert == owner * EXP_DEV + j, 1.0, 0.0).astype(BF16)


def chosen_of(spread, hits, earlier):
    shape = (spread.shape[0], hits.shape[1])
    slot = (lax.broadcasted_iota(jnp.int32, shape, 0) % SLOTS).astype(F32)
    return (dot(spread, hits) > 0.5) & (dot(spread, earlier) == slot)


def counts_of(ids, experts):
    rows = ids.shape[1]
    line = lax.broadcasted_iota(jnp.int32, (experts, rows), 0)
    hits = jnp.zeros((experts, rows), F32)
    for k in range(TOPK):
        hits = hits + jnp.where(ids[k : k + 1, :] == line, 1.0, 0.0)
    before = lax.broadcasted_iota(jnp.int32, (rows, rows), 0) < lax.broadcasted_iota(
        jnp.int32, (rows, rows), 1
    )
    hits = hits.astype(BF16)
    return hits, dot(hits, jnp.where(before, 1.0, 0.0).astype(BF16)).astype(BF16)


def weigh_kernel(ids_ref, probs_ref, place_ref, *tables):
    slots, rows = place_ref.shape
    experts = EXP_DEV * slots // SLOTS
    ids, probs = ids_ref[...], probs_ref[...]
    hits, earlier = counts_of(ids, experts)
    mix = probs / jnp.sum(probs, axis=0, keepdims=True)
    line = lax.broadcasted_iota(jnp.int32, hits.shape, 0)
    mixed = jnp.zeros(hits.shape, F32)
    for k in range(TOPK):
        mixed = mixed + jnp.where(ids[k : k + 1, :] == line, mix[k : k + 1, :], 0.0)
    mix_hi = mixed.astype(BF16)
    mix_lo = (mixed - mix_hi.astype(F32)).astype(BF16)
    for j in range(EXP_DEV):
        spread = spread_of(slots, experts, j)
        chosen = chosen_of(spread, hits, earlier)
        tables[j][...] = jnp.where(chosen, dot(spread, mix_hi), 0.0).astype(BF16)
        tables[2 + j][...] = jnp.where(chosen, dot(spread, mix_lo), 0.0).astype(BF16)
        if j == 1:
            place_ref[...] = jnp.where(chosen, 1.0, 0.0).astype(BF16)


def weigh(ids, probs, devices, after):
    table = jax.ShapeDtypeStruct((devices * SLOTS, ids.shape[1]), BF16)

    def kernel(ids_ref, probs_ref, _, *tables):
        weigh_kernel(ids_ref, probs_ref, *tables)

    return pl.pallas_call(
        kernel,
        in_specs=[VMEM, VMEM, ANY],
        out_specs=[VMEM] * 5,
        out_shape=[table] * 5,
        name="weigh",
    )(ids, probs, after)


def split_columns(me, w):
    count, hidden, width = w.shape
    part = width // N_TP
    block = pl.BlockSpec((count, hidden // 2, part), lambda h, m: (0, h, 0))

    def kernel(me_ref, w_ref, *out_refs):
        for turn, out_ref in enumerate(out_refs):
            out_ref[...] = w_ref[:, :, columns(me_ref, turn + 1, part)]

    return pl.pallas_call(
        kernel,
        grid_spec=pltpu.PrefetchScalarGridSpec(
            num_scalar_prefetch=1,
            grid=(2,),
            in_specs=[pl.BlockSpec((count, hidden // 2, width), lambda h, m: (0, h, 0))],
            out_specs=[block] * (N_TP - 1),
        ),
        out_shape=[jax.ShapeDtypeStruct((count, hidden, part), w.dtype)] * (N_TP - 1),
        compiler_params=BIG,
        cost_estimate=pl.CostEstimate(flops=0, bytes_accessed=4 * w.size, transcendentals=0),
        name="split_columns",
    )(me, w)


def attention_kernel(
    lens_ref, q_ref, nk_ref, nv_ref, k_ref, v_ref, res_ref, gain_ref, ids_ref,
    summed_ref, scaled_ref, placed_ref, table, held
):
    rows, span, depth = k_ref.shape
    heads = q_ref.shape[1] // depth
    base = pl.program_id(0) * rows
    lines = rows * heads
    q = q_ref[...].astype(F32).reshape(rows, heads, depth)
    qb = q.astype(BF16)
    dims = (((1,), (1,)), ((), ()))
    scores = jnp.concatenate(
        [
            lax.dot_general(qb[r], k_ref[r], dims, preferred_element_type=F32)
            for r in range(rows)
        ],
        axis=0,
    )
    scale = 1.0 / math.sqrt(depth)
    line = lax.broadcasted_iota(jnp.int32, (lines, span), 0) // heads
    limit = jnp.zeros((lines, span), jnp.int32)
    for r in range(rows):
        limit = jnp.where(line == r, lens_ref[base + r], limit)
    live = lax.broadcasted_iota(jnp.int32, (lines, span), 1) < limit
    scores = jnp.where(live, scores * scale, -jnp.inf)
    fresh_key = jnp.broadcast_to(nk_ref[...].astype(F32)[:, None, :], (rows, heads, depth))
    fresh = jnp.sum(q * fresh_key, axis=2, keepdims=True).reshape(lines, 1) * scale
    top = jnp.maximum(jnp.max(scores, axis=1, keepdims=True), fresh)
    exps = jnp.exp(scores - top)
    fresh_exp = jnp.exp(fresh - top)
    total = jnp.sum(exps, axis=1, keepdims=True) + fresh_exp
    weights = (exps / total).astype(BF16)
    fresh_weight = (fresh_exp / total).astype(BF16).astype(F32)
    fresh_value = jnp.broadcast_to(nv_ref[...].astype(F32)[:, None, :], (rows, heads, depth))
    out = jnp.concatenate(
        [dot(weights[r * heads : (r + 1) * heads], v_ref[r]) for r in range(rows)], axis=0
    )
    out = out + fresh_weight * fresh_value.reshape(lines, depth)
    summed = res_ref[...].astype(F32) + out.reshape(rows, heads, depth).reshape(
        rows, heads * depth
    )
    summed_ref[...] = summed
    scaled = (summed * gain_ref[...]).astype(BF16)
    scaled_ref[...] = scaled
    held[pl.ds(pl.multiple_of(base, rows), rows), :] = scaled

    @pl.when(pl.program_id(0) == 0)
    def _():
        slots = table.shape[0]
        experts = EXP_DEV * slots // SLOTS
        hits, earlier = counts_of(ids_ref[...], experts)
        chosen = chosen_of(spread_of(slots, experts, 0), hits, earlier)
        table[...] = jnp.where(chosen, 1.0, 0.0).astype(BF16)

    @pl.when(pl.program_id(0) == pl.num_programs(0) - 1)
    def _():
        placed_ref[...] = dot(table[...], held[...]).astype(BF16)


def attention(lens, me, queries, new_key, new_value, keys, values, residual, gain, ids, devices):
    rows, part = queries.shape
    span, depth = keys.shape[1:]
    step = 32
    wide = pl.BlockSpec((step, part), lambda i, n, m: (i, 0))
    slim = pl.BlockSpec((step, depth), lambda i, n, m: (i, 0))
    cache = pl.BlockSpec((step, span, depth), lambda i, n, m: (i, 0, 0))

    def kernel(lens_ref, me_ref, *refs):
        attention_kernel(lens_ref, *refs)

    return pl.pallas_call(
        kernel,
        grid_spec=pltpu.PrefetchScalarGridSpec(
            num_scalar_prefetch=2,
            grid=(rows // step,),
            in_specs=[wide, slim, slim, cache, cache, wide,
                      pl.BlockSpec((1, part), lambda i, n, m: (0, m[0])),
                      pl.BlockSpec(ids.shape, lambda i, n, m: (0, 0))],
            out_specs=[wide, wide,
                       pl.BlockSpec((devices * SLOTS, part), lambda i, n, m: (0, 0))],
            scratch_shapes=[
                pltpu.VMEM((devices * SLOTS, rows), BF16), pltpu.VMEM((rows, part), BF16)
            ],
        ),
        out_shape=[
            jax.ShapeDtypeStruct((rows, part), F32),
            jax.ShapeDtypeStruct((rows, part), BF16),
            jax.ShapeDtypeStruct((devices * SLOTS, part), BF16),
        ],
        compiler_params=pltpu.CompilerParams(vmem_limit_bytes=58 << 20),
        cost_estimate=pl.CostEstimate(
            flops=4 * rows * part * span,
            bytes_accessed=4 * rows * span * depth,
            transcendentals=rows * part,
        ),
        name="attention",
    )(lens, me, queries, new_key, new_value, keys, values, residual, gain, ids)


def place_kernel(table_ref, rows_ref, *refs):
    refs[-1][...] = dot(table_ref[...], rows_ref[...]).astype(BF16)


def place_rows(table, rows, *after):
    slots, part = table.shape[0], rows.shape[1]
    return pl.pallas_call(
        place_kernel,
        grid=(2,),
        in_specs=[
            pl.BlockSpec((slots // 2, table.shape[1]), lambda i: (i, 0)),
            pl.BlockSpec(rows.shape, lambda i: (0, 0)),
        ]
        + [ANY] * len(after),
        out_specs=pl.BlockSpec((slots // 2, part), lambda i: (i, 0)),
        out_shape=jax.ShapeDtypeStruct((slots, part), BF16),
        cost_estimate=pl.CostEstimate(
            flops=2 * table.size * part, bytes_accessed=4 * slots * part, transcendentals=0
        ),
        name="place_rows",
    )(table, rows, *after)


def pick_kernel(all_ref, *refs):
    for i, out_ref in enumerate(refs[-2:]):
        count = all_ref.shape[0] // 2
        out_ref[...] = all_ref[pl.ds(i * count, count)].reshape(out_ref.shape)


def pick(everything, expert, work, *after):
    devices, _, slots, part = everything.shape
    half = devices * slots // 2
    return pl.pallas_call(
        pick_kernel,
        grid=(1,),
        in_specs=[pl.BlockSpec((devices, 1, slots, part), lambda i: (0, expert, 0, 0))]
        + [ANY] * len(after),
        out_specs=[pl.BlockSpec((half, part), lambda i: (0, 0))] * 2,
        out_shape=[jax.ShapeDtypeStruct((half, part), everything.dtype)] * 2,
        compiler_params=BIG,
        cost_estimate=pl.CostEstimate(
            flops=int(work * 1e9), bytes_accessed=8 * half * part, transcendentals=0
        ),
        name="pick",
    )(everything, *after)


def in_hbm(*arrays):
    return [pltpu.with_memory_space_constraint(array, pltpu.HBM) for array in arrays]


def exchange(for_right, for_across, for_left):
    return (
        lax.ppermute(for_right, "tp", RIGHT),
        lax.ppermute(for_left, "tp", LEFT),
        lax.ppermute(for_across, "tp", ACROSS),
    )


def columns(me_ref, turn, part):
    return pl.ds(pl.multiple_of(lax.rem(me_ref[0] + turn, N_TP) * part, part), part)


def project(x, cols, gate_ref, up_ref, inv_ref):
    dims = (((1,), (1,)), ((), ()))
    plain = x.astype(F32) * inv_ref[:, cols]
    return (
        lax.dot_general(x, gate_ref[0, :, cols], dims, preferred_element_type=F32),
        lax.dot_general(x, up_ref[0, :, cols], dims, preferred_element_type=F32),
        jnp.sum(plain * plain, axis=1, keepdims=True),
    )


def near_kernel(
    me_ref, own0, own1, left0, left1, right0, right1, gate_ref, up_ref, inv_ref,
    gate_out, up_out, sq_out,
):
    half, part = own0.shape
    for i, blocks in enumerate(((own0, left0, right0), (own1, left1, right1))):
        rows = pl.ds(i * half, half)
        total = None
        for block, turn in zip(blocks, (0, N_TP - 1, 1), strict=True):
            term = project(block[...], columns(me_ref, turn, part), gate_ref, up_ref, inv_ref)
            total = term if total is None else tuple(
                a + b for a, b in zip(total, term, strict=True)
            )
        gate_out[rows, :], up_out[rows, :] = total[0], total[1]
        sq_out[rows, :] = jnp.broadcast_to(total[2], (half, sq_out.shape[1]))


def far_kernel(me_ref, low, high, gate_in, up_in, sq_in, gate_ref, up_ref, inv_ref, out_ref):
    half, part = low.shape
    hidden = gate_in.shape[1]
    tails = []
    for i, block in enumerate((low, high)):
        rows = slice(i * half, (i + 1) * half)
        cols = pl.ds(0, part)
        gate, up, squares = project(block[...], cols, gate_ref, up_ref, inv_ref)
        scale = lax.rsqrt((sq_in[rows, :1] + squares) / (N_TP * part) + epsilon)
        gate, up = (gate_in[rows] + gate) * scale, (up_in[rows] + up) * scale
        value = gate / (1.0 + jnp.exp(-gate)) * up
        out_ref[rows, :] = value[:, :128].astype(BF16)
        tails.append(value[:, 128:hidden])
    out_ref[2 * half :, :] = jnp.concatenate(tails, axis=1).astype(BF16)


def near_project(me, blocks, w_gate, w_up, inv_gain, expert):
    rows, part = 2 * blocks[0].shape[0], blocks[0].shape[1]
    hidden, width = w_gate.shape[1:]

    def whole(shape):
        return pl.BlockSpec(shape, lambda i, m: (0,) * len(shape))

    weight = pl.BlockSpec((1, hidden, width), lambda i, m: (expert, 0, 0))
    return pl.pallas_call(
        near_kernel,
        grid_spec=pltpu.PrefetchScalarGridSpec(
            num_scalar_prefetch=1,
            grid=(1,),
            in_specs=[whole(blocks[0].shape)] * 6 + [weight, weight, whole((1, width))],
            out_specs=[whole((rows, hidden)), whole((rows, hidden)), whole((rows, 128))],
        ),
        out_shape=[jax.ShapeDtypeStruct((rows, hidden), F32)] * 2
        + [jax.ShapeDtypeStruct((rows, 128), F32)],
        compiler_params=pltpu.CompilerParams(vmem_limit_bytes=32 << 20),
        cost_estimate=pl.CostEstimate(
            flops=3 * rows * width * hidden,
            bytes_accessed=2 * rows * width + 4 * hidden * width,
            transcendentals=0,
        ),
        name="near_project",
    )(me, *blocks, w_gate, w_up, inv_gain)


def far_project(me, low, high, near, w_gate, w_up, inv_gain, expert, weight_us):
    half, part = low.shape
    hidden, width = w_gate.shape[1:]
    rows = 2 * half

    def whole(shape):
        return pl.BlockSpec(shape, lambda i, m: (0,) * len(shape))

    def across(m):
        return lax.rem(m[0] + 2, N_TP)

    weight = pl.BlockSpec((1, hidden, part), lambda i, m: (expert, 0, across(m)))
    packed = (rows + rows * (hidden - 128) // 128, 128)

    return pl.pallas_call(
        far_kernel,
        grid_spec=pltpu.PrefetchScalarGridSpec(
            num_scalar_prefetch=1,
            grid=(1,),
            in_specs=[whole(low.shape), whole(high.shape)]
            + [whole(a.shape) for a in near]
            + [weight, weight, pl.BlockSpec((1, part), lambda i, m: (0, across(m)))],
            out_specs=whole(packed),
        ),
        out_shape=jax.ShapeDtypeStruct(packed, BF16),
        compiler_params=BIG,
        cost_estimate=pl.CostEstimate(
            flops=int(weight_us * 1e9), bytes_accessed=8 * rows * part, transcendentals=0
        ),
        name="far_project",
    )(me, low, high, *near, w_gate, w_up, inv_gain)


def down_kernel(me_ref, h0, h1, h2, h3, w0, w1, w2, w3, out_ref, *plain):
    rows, hidden = plain[0].shape

    @pl.when(pl.program_id(0) == 0)
    def _():
        for packed, full in zip((h0, h1, h2, h3), plain, strict=True):
            tails = packed[rows:, :]
            full[:, :128] = packed[:rows, :]
            full[: rows // 2, 128:] = tails[:, : hidden - 128]
            full[rows // 2 :, 128:] = tails[:, hidden - 128 :]

    total = None
    for full, w_ref in zip(plain, (w0, w1, w2, w3), strict=True):
        term = dot(full[...], w_ref[0])
        total = term if total is None else total + term
    out_ref[...] = total.astype(out_ref.dtype)


def down_project(me, packed, w_down, moved, rows, expert, *after):
    _, hidden, part = moved[0].shape
    whole = pl.BlockSpec(packed[0].shape, lambda i, m: (0, 0))
    steps = 1
    piece = part // steps
    own = pl.BlockSpec((1, hidden, piece), lambda i, m: (expert, 0, m[0] * steps + i))
    other = pl.BlockSpec((1, hidden, piece), lambda i, m: (expert, 0, i))

    def kernel(*refs):
        head = 1 + 2 * N_TP
        down_kernel(*refs[:head], *refs[head + len(after) :])

    return pl.pallas_call(
        kernel,
        grid_spec=pltpu.PrefetchScalarGridSpec(
            num_scalar_prefetch=1,
            grid=(steps,),
            in_specs=[whole] * N_TP + [own] + [other] * (N_TP - 1) + [ANY] * len(after),
            out_specs=pl.BlockSpec((rows, piece), lambda i, m: (0, i)),
            scratch_shapes=[pltpu.VMEM((rows, hidden), BF16)] * N_TP,
        ),
        out_shape=pltpu.HBM((rows, part), BF16),
        compiler_params=BIG,
        cost_estimate=pl.CostEstimate(
            flops=8 * rows * hidden * part,
            bytes_accessed=8 * rows * hidden + 8 * hidden * part + 2 * rows * part,
            transcendentals=0,
        ),
        name="down_project",
    )(me, *packed, w_down, *moved, *after)


def mix_kernel(total_ref, hi_ref, lo_ref, back_ref, out_ref):
    back = back_ref[...]
    total = total_ref[...].astype(F32)
    for weight in (hi_ref, lo_ref):
        total = total + dot(weight[...], back)
    out_ref[...] = total.astype(out_ref.dtype)


def mix_in(total, hi, lo, back, dtype):
    rows, part = total.shape
    steps = 2
    column = pl.BlockSpec((rows, part // steps), lambda i: (0, i))
    weight = pl.BlockSpec(hi.shape, lambda i: (0, 0))
    return pl.pallas_call(
        mix_kernel,
        grid=(steps,),
        in_specs=[column, weight, weight,
                  pl.BlockSpec((back.shape[0], part // steps), lambda i: (0, i))],
        out_specs=column,
        out_shape=jax.ShapeDtypeStruct((rows, part), dtype),
        compiler_params=BIG,
        cost_estimate=pl.CostEstimate(
            flops=4 * hi.size * part, bytes_accessed=2 * back.size, transcendentals=0
        ),
        name="mix_in",
    )(total, hi, lo, back)


def body(
    queries, new_key, new_value, key_cache, value_cache, cache_len, residual,
    norm_gain, expert_ids, gate_probs, w_gate, w_up, w_down,
):
    rows, part = residual.shape
    group = ("side", "grp")
    devices = lax.axis_size("side") * lax.axis_size("grp")
    slots = devices * SLOTS
    me = lax.axis_index("tp").astype(jnp.int32).reshape(1)
    blocks = split_columns(me, w_down)
    gain = norm_gain.reshape(1, -1)
    inv_gain = 1.0 / gain
    ids = expert_ids.T
    summed, scaled, placed0 = attention(
        cache_len, me, queries, new_key, new_value, key_cache, value_cache, residual, gain,
        ids, devices,
    )
    table1, hi0, hi1, lo0, lo1 = weigh(ids, gate_probs.T, devices, blocks[0])
    swap = functools.partial(
        lax.all_to_all, axis_name=group, split_axis=0, concat_axis=0, tiled=True
    )
    moved = in_hbm(*exchange(*blocks))
    w_gate, w_up = in_hbm(w_gate, w_up)
    total = summed
    own = ()
    for expert, hi, lo in ((0, hi0, lo0), (1, hi1, lo1)):
        placed = place_rows(table1, scaled) if expert else placed0
        arrived = swap(placed.reshape(devices, SLOTS, part)).reshape(devices, 1, SLOTS, part)
        own = pick(arrived, 0, PICK_WEIGHT[expert], *moved[: 3 * expert])
        left = [lax.ppermute(half, "tp", RIGHT) for half in own]
        right = [lax.ppermute(half, "tp", LEFT) for half in own]
        low = lax.ppermute(left[0], "tp", RIGHT)
        high = lax.ppermute(right[1], "tp", LEFT)
        sums = near_project(me, (*own, *left, *right), w_gate, w_up, inv_gain, expert)
        packed = far_project(
            me, low, high, sums, w_gate, w_up, inv_gain, expert, FAR_WEIGHT[expert]
        )
        packed = packed, *exchange(packed, packed, packed)
        produced = down_project(me, packed, w_down, moved, slots, expert)
        back = swap(produced.reshape(devices, SLOTS, part)).reshape(slots, part)
        total = mix_in(total, hi.T, lo.T, back, F32 if expert == 0 else BF16)
    return total


def solution(mesh):
    in_specs = (
        P(("side", "grp"), "tp"),
        P(("side", "grp"), "tp"),
        P(("side", "grp"), "tp"),
        P(("side", "grp"), None, "tp"),
        P(("side", "grp"), None, "tp"),
        P(("side", "grp")),
        P(("side", "grp"), "tp"),
        P(),
        P(("side", "grp"), None),
        P(("side", "grp"), None),
        P(("side", "grp"), "tp", None),
        P(("side", "grp"), "tp", None),
        P(("side", "grp"), "tp", None),
    )
    out_specs = P(("side", "grp"), "tp")
    return jax.shard_map(body, mesh=mesh, in_specs=in_specs, out_specs=out_specs, check_vma=False)
```
